32 devices in a mesh: rep: 8 (over z, x), shard: 4 (over y, core).
Axes of the slice: x: 2, y: 2, z: 4, core: 2. Of those that a mesh axis runs over, the one named last changes fastest.
Arguments:
- hidden_in: bfloat16 [8, 512, 960], P('rep', 'shard'), may hold values from -6 to 6
- out_grad: bfloat16 [8, 512, 960], P('rep', 'shard'), may hold values from -6 to 6
- norm1_gain: bfloat16 [960], P('shard'), may hold values from 0.5 to 1.5
- q_weight: bfloat16 [960, 960], P('shard'), may hold values from -0.1875 to 0.1875
- k_weight: bfloat16 [960, 320], P('shard'), may hold values from -0.1875 to 0.1875
- v_weight: bfloat16 [960, 320], P('shard'), may hold values from -0.1875 to 0.1875
- o_weight: bfloat16 [960, 960], P(None, 'shard'), may hold values from -1.5 to 1.5
- norm2_gain: bfloat16 [960], P('shard'), may hold values from 0.5 to 1.5
- gate_weight: bfloat16 [960, 2560], P('shard'), may hold values from -0.1875 to 0.1875
- up_weight: bfloat16 [960, 2560], P('shard'), may hold values from -0.1875 to 0.1875
- down_weight: bfloat16 [2560, 960], P('shard'), may hold values from -0.125 to 0.125
Outputs:
- output: float32 [8, 512, 960], P('rep', 'shard')
- input_grad: float32 [8, 512, 960], P('rep', 'shard')
- norm1_gain_grad: float32 [960], P('shard')
- q_weight_grad: float32 [960, 960], P('shard')
- k_weight_grad: float32 [960, 320], P('shard')
- v_weight_grad: float32 [960, 320], P('shard')
- o_weight_grad: float32 [960, 960], P(None, 'shard')
- norm2_gain_grad: float32 [960], P('shard')
- gate_weight_grad: float32 [960, 2560], P('shard')
- up_weight_grad: float32 [960, 2560], P('shard')
- down_weight_grad: float32 [2560, 960], P('shard')
The draws below stay inside these ranges and needn't reach their ends.
All inputs are finite; a program needn't handle non-finite values.
Results may differ from the reference program's by a relative error of at most 0.02.
Values may be sent and summed in bfloat16 or wider, within the bound.
No kernel may reach another device: no remote copies, remote signals or barrier semaphores. Data moves between devices by JAX's collectives and lax.ppermute only.
A program may use at most 192 MiB of HBM per device.

```python
from functools import partial
import jax
import jax.numpy as jnp
from jax import lax

D = 960
HQ = 15
KEY_VALUE_HEADS = 5
HEAD_SIZE = 64
FF = 2560
QD = 960
KVD = 320
QUERY_PER_KV = 3
SEQ_LEN = 512
SEQS = 8


def levels(own_key, dims, shards, smallest, largest):
    gain, own = 1.0, jax.random.fold_in(own_key, 6)
    for axis_at, blocks in shards:
        steps = jnp.exp(jax.random.uniform(jax.random.fold_in(own, axis_at), (blocks,), jnp.float32, smallest / len(shards), largest / len(shards)))
        gain = gain * jnp.repeat(steps, dims[axis_at] // blocks).reshape([-1 if axis == axis_at else 1 for axis in range(len(dims))])
    return gain


def noise(stream_key, extent, scale, reach, split=(), kind=jnp.bfloat16):
    drawn = jax.random.normal(stream_key, extent, jnp.float32) * scale
    if len(split) > 0:
        drawn = levels(stream_key, extent, split, -0.22, 0.18) * drawn
    return jnp.clip(drawn, min=-reach, max=reach).astype(kind)


def setup_inputs(seed: int = 0) -> dict:
    splits = jax.random.split(jax.random.key(seed), 12)
    hidden_in = noise(splits[0], (SEQS, SEQ_LEN, D), 1.0, 6.0, ((0, 8), (1, 4)))
    out_grad = noise(splits[1], (SEQS, SEQ_LEN, D), 1.0, 6.0, ((0, 8), (1, 4)))
    norm1_gain = jnp.clip(1.0 + 0.1 * jax.random.normal(splits[2], (D,), jnp.float32), 0.5, 1.5).astype(jnp.bfloat16)
    q_weight = noise(splits[3], (D, QD), D ** -0.5, 0.1875, ((0, 4),))
    k_weight = noise(splits[4], (D, KVD), D ** -0.5, 0.1875, ((0, 4),))
    v_weight = noise(splits[5], (D, KVD), D ** -0.5, 0.1875, ((0, 4),))
    o_weight = noise(splits[6], (QD, D), (QD // 64) ** -0.5, 1.5, ((1, 4),))
    norm2_gain = jnp.clip(1.0 + 0.1 * jax.random.normal(splits[7], (D,), jnp.float32), 0.5, 1.5).astype(jnp.bfloat16)
    gate_weight = noise(splits[8], (D, FF), D ** -0.5, 0.1875, ((0, 4),))
    up_weight = noise(splits[9], (D, FF), D ** -0.5, 0.1875, ((0, 4),))
    down_weight = noise(splits[10], (FF, D), FF ** -0.5, 0.125, ((0, 4),))
    return {"hidden_in": hidden_in, "out_grad": out_grad, "norm1_gain": norm1_gain, "q_weight": q_weight, "k_weight": k_weight, "v_weight": v_weight, "o_weight": o_weight, "norm2_gain": norm2_gain, "gate_weight": gate_weight, "up_weight": up_weight, "down_weight": down_weight}


EPSILON = 1e-05
SCALE = 0.125
NEGATIVE = -1e+30
THETA = 10000.0

def rms_inverse(rows):
    return lax.rsqrt(lax.optimization_barrier(jnp.mean(rows * rows, axis=-1, keepdims=True)) + EPSILON)

def rope_tables(positions):
    half = HEAD_SIZE // 2
    freqs = THETA ** (-(jnp.arange(half, dtype=jnp.float32) * 2.0 / HEAD_SIZE))
    angles = positions.astype(jnp.float32)[:, None] * freqs[None, :]
    return (jnp.cos(angles)[:, None, :], jnp.sin(angles)[:, None, :])

def rotate(tensor, cosine_table, sine_table):
    half = HEAD_SIZE // 2
    first, second = (tensor[..., :half], tensor[..., half:])
    return jnp.concatenate([first * cosine_table - second * sine_table, second * cosine_table + first * sine_table], axis=-1)

def inverse_rotary(tensor, cosine_table, sine_table):
    half = HEAD_SIZE // 2
    first, second = (tensor[..., :half], tensor[..., half:])
    return jnp.concatenate([first * cosine_table + second * sine_table, second * cosine_table - first * sine_table], axis=-1)

def head_scores(query_rows, keys, query_pos, key_pos):
    scores = jnp.einsum('ngd,ld->gnl', query_rows.astype(jnp.float32), keys.astype(jnp.float32)) * SCALE
    allowed = key_pos[None, None, :] <= query_pos[None, :, None]
    return (jnp.where(allowed, scores, NEGATIVE), allowed)

def head_forward(inputs, query_pos, key_pos):
    query_rows, keys, value_rows = inputs
    scores, allowed = head_scores(query_rows, keys, query_pos, key_pos)
    log_total = jax.nn.logsumexp(scores, axis=-1)
    probs = jnp.where(allowed, jnp.exp(scores - log_total[..., None]), 0.0)
    probs_b = probs.astype(jnp.bfloat16)
    attended_rows = jnp.einsum('gnl,ld->ngd', probs_b.astype(jnp.float32), value_rows.astype(jnp.float32))
    return (attended_rows, log_total)

def head_backward(inputs, query_pos, key_pos):
    query_rows, keys, value_rows, log_total, attention_gradient, attended_rows = inputs
    scores, allowed = head_scores(query_rows, keys, query_pos, key_pos)
    probs = jnp.where(allowed, jnp.exp(scores - log_total[..., None]), 0.0)
    probs_b = probs.astype(jnp.bfloat16).astype(jnp.float32)
    grad_att_f = attention_gradient.astype(jnp.float32)
    value_grad = jnp.einsum('gnl,ngd->ld', probs_b, grad_att_f)
    grad_prob = jnp.einsum('ngd,ld->gnl', grad_att_f, value_rows.astype(jnp.float32))
    delta = jnp.transpose(lax.optimization_barrier(jnp.sum(grad_att_f * attended_rows.astype(jnp.float32), axis=-1)))
    grad_score = (probs * (grad_prob - delta[..., None]) * SCALE).astype(jnp.bfloat16).astype(jnp.float32)
    query_grad = jnp.einsum('gnl,ld->ngd', grad_score, keys.astype(jnp.float32))
    key_grad = jnp.einsum('gnl,ngd->ld', grad_score, query_rows.astype(jnp.float32))
    return (query_grad, key_grad, value_grad)

def outer(left, right):
    return lax.dot_general(left, right, (((0,), (0,)), ((), ())), preferred_element_type=jnp.float32)

def back(left, weight):
    return lax.dot_general(left, weight, (((1,), (1,)), ((), ())), preferred_element_type=jnp.float32)

def layer_pass(hidden, cotangent, params, positions):
    gain_one, w_query, key_matrix, value_matrix, w_out, gain_two, w_gate, w_up, w_down = params
    token_count = hidden.shape[0]
    x_full = hidden.astype(jnp.float32)
    inv_one = rms_inverse(x_full)
    normed_one = x_full * inv_one
    gain_one_f = gain_one.astype(jnp.float32)
    first_input = (normed_one * gain_one_f).astype(jnp.bfloat16)
    cosine_table, sine_table = rope_tables(positions)
    query_raw = jnp.dot(first_input, w_query, preferred_element_type=jnp.float32).reshape(token_count, HQ, HEAD_SIZE)
    query_rows = rotate(query_raw, cosine_table, sine_table).astype(jnp.bfloat16)
    unrotated_key = jnp.dot(first_input, key_matrix, preferred_element_type=jnp.float32).reshape(token_count, KEY_VALUE_HEADS, HEAD_SIZE)
    keys = rotate(unrotated_key, cosine_table, sine_table).astype(jnp.bfloat16)
    value_rows = jnp.dot(first_input, value_matrix, preferred_element_type=jnp.float32).astype(jnp.bfloat16).reshape(token_count, KEY_VALUE_HEADS, HEAD_SIZE)
    query_head_rows = jnp.transpose(query_rows.reshape(token_count, KEY_VALUE_HEADS, QUERY_PER_KV, HEAD_SIZE), (1, 0, 2, 3))
    key_head_rows = jnp.transpose(keys, (1, 0, 2))
    value_head_rows = jnp.transpose(value_rows, (1, 0, 2))
    att_heads, log_total = lax.map(partial(head_forward, query_pos=positions, key_pos=positions), (query_head_rows, key_head_rows, value_head_rows))
    attended_rows = jnp.transpose(att_heads, (1, 0, 2, 3)).reshape(token_count, QD).astype(jnp.bfloat16)
    x_one = x_full + jnp.dot(attended_rows, w_out, preferred_element_type=jnp.float32)
    inv_two = rms_inverse(x_one)
    normed_two = x_one * inv_two
    gain_two_f = gain_two.astype(jnp.float32)
    input_two = (normed_two * gain_two_f).astype(jnp.bfloat16)
    gate = jnp.dot(input_two, w_gate, preferred_element_type=jnp.float32)
    upward = jnp.dot(input_two, w_up, preferred_element_type=jnp.float32)
    sigma = jax.nn.sigmoid(gate)
    silu_gate = gate * sigma
    hidden_act = (silu_gate * upward).astype(jnp.bfloat16)
    output = x_one + jnp.dot(hidden_act, w_down, preferred_element_type=jnp.float32)
    grad_down = outer(hidden_act, cotangent)
    grad_hidden = back(cotangent, w_down)
    grad_gate = (grad_hidden * upward * sigma * (1.0 + gate * (1.0 - sigma))).astype(jnp.bfloat16)
    grad_upward = (grad_hidden * silu_gate).astype(jnp.bfloat16)
    grad_wgate = outer(input_two, grad_gate)
    grad_wup = outer(input_two, grad_upward)
    grad_in_two = back(grad_gate, w_gate) + back(grad_upward, w_up)
    grad_gain_two = lax.optimization_barrier(jnp.sum(grad_in_two * normed_two, axis=0))
    grad_norm_two = grad_in_two * gain_two_f
    grad_x_one = cotangent.astype(jnp.float32) + inv_two * (grad_norm_two - normed_two * lax.optimization_barrier(jnp.mean(grad_norm_two * normed_two, axis=-1, keepdims=True)))
    grad_x_one_b = grad_x_one.astype(jnp.bfloat16)
    grad_wout = outer(attended_rows, grad_x_one_b)
    attention_gradient = back(grad_x_one_b, w_out).astype(jnp.bfloat16)
    attention_head_gradient = jnp.transpose(attention_gradient.reshape(token_count, KEY_VALUE_HEADS, QUERY_PER_KV, HEAD_SIZE), (1, 0, 2, 3))
    attention_heads_bf16 = jnp.transpose(attended_rows.reshape(token_count, KEY_VALUE_HEADS, QUERY_PER_KV, HEAD_SIZE), (1, 0, 2, 3))
    q_grad, k_grad, v_grad = lax.map(partial(head_backward, query_pos=positions, key_pos=positions), (query_head_rows, key_head_rows, value_head_rows, log_total, attention_head_gradient, attention_heads_bf16))
    query_grad = jnp.transpose(q_grad, (1, 0, 2, 3)).reshape(token_count, HQ, HEAD_SIZE)
    key_grad = jnp.transpose(k_grad, (1, 0, 2))
    value_grad = jnp.transpose(v_grad, (1, 0, 2))
    grad_q = inverse_rotary(query_grad, cosine_table, sine_table).reshape(token_count, QD).astype(jnp.bfloat16)
    grad_k = inverse_rotary(key_grad, cosine_table, sine_table).reshape(token_count, KVD).astype(jnp.bfloat16)
    grad_v = value_grad.reshape(token_count, KVD).astype(jnp.bfloat16)
    grad_wquery = outer(first_input, grad_q)
    grad_wkey = outer(first_input, grad_k)
    grad_wvalue = outer(first_input, grad_v)
    grad_in_one = back(grad_q, w_query) + back(grad_k, key_matrix) + back(grad_v, value_matrix)
    grad_gain_one = lax.optimization_barrier(jnp.sum(grad_in_one * normed_one, axis=0))
    grad_norm_one = grad_in_one * gain_one_f
    grad_input = grad_x_one + inv_one * (grad_norm_one - normed_one * lax.optimization_barrier(jnp.mean(grad_norm_one * normed_one, axis=-1, keepdims=True)))
    grads = (grad_gain_one, grad_wquery, grad_wkey, grad_wvalue, grad_wout, grad_gain_two, grad_wgate, grad_wup, grad_down)
    return (output, grad_input, grads)

def reference(hidden_in, out_grad, norm1_gain, q_weight, k_weight, v_weight, o_weight, norm2_gain, gate_weight, up_weight, down_weight):
    params = (norm1_gain, q_weight, k_weight, v_weight, o_weight, norm2_gain, gate_weight, up_weight, down_weight)
    positions = jnp.arange(SEQ_LEN, dtype=jnp.int32)
    starting = tuple((jnp.zeros(param.shape, jnp.float32) for param in params))

    def one_sequence(running, pieces):
        output, grad_input, grads = layer_pass(pieces[0], pieces[1], params, positions)
        return (tuple((total + grad for total, grad in zip(running, grads))), (output, grad_input))
    totals, (outputs, input_grads) = lax.scan(one_sequence, starting, (hidden_in, out_grad))
    return (outputs, input_grads, totals[0], totals[1], totals[2], totals[3], totals[4], totals[5], totals[6], totals[7], totals[8])
```

```python
from functools import partial

import jax
import jax.numpy as jnp
from jax import lax
from jax.sharding import PartitionSpec as P

HEAD_SIZE = 64
QUERY_PER_KV = 3
EPSILON = 1e-05
SCALE = 0.125
NEGATIVE = -1e30
THETA = 10000.0
BF = jnp.bfloat16
F32 = jnp.float32


def rms_inverse(rows):
    return lax.rsqrt(jnp.mean(rows * rows, axis=-1, keepdims=True) + EPSILON)


def rope_tables(positions):
    half = HEAD_SIZE // 2
    freqs = THETA ** (-(jnp.arange(half, dtype=F32) * 2.0 / HEAD_SIZE))
    angles = positions.astype(F32)[:, None] * freqs[None, :]
    return (jnp.cos(angles)[:, None, :], jnp.sin(angles)[:, None, :])


def rotate(tensor, cosine_table, sine_table):
    half = HEAD_SIZE // 2
    first, second = (tensor[..., :half], tensor[..., half:])
    return jnp.concatenate(
        [first * cosine_table - second * sine_table, second * cosine_table + first * sine_table],
        axis=-1,
    )


def head_scores(query_rows, keys, query_pos, key_pos):
    scores = jnp.einsum("ngd,ld->gnl", query_rows, keys, preferred_element_type=F32) * SCALE
    allowed = key_pos[None, None, :] <= query_pos[None, :, None]
    return (jnp.where(allowed, scores, NEGATIVE), allowed)


def head_forward(inputs, query_pos, key_pos):
    query_rows, keys, value_rows = inputs
    scores, allowed = head_scores(query_rows, keys, query_pos, key_pos)
    log_total = jax.nn.logsumexp(scores, axis=-1)
    probs = jnp.where(allowed, jnp.exp(scores - log_total[..., None]), 0.0)
    attended_rows = jnp.einsum(
        "gnl,ld->ngd", probs.astype(BF), value_rows, preferred_element_type=F32
    )
    return (attended_rows, log_total)


def head_backward(inputs, query_pos, key_pos):
    query_rows, keys, value_rows, log_total, attention_gradient, attended_rows = inputs
    scores, allowed = head_scores(query_rows, keys, query_pos, key_pos)
    probs = jnp.where(allowed, jnp.exp(scores - log_total[..., None]), 0.0)
    probs_b = probs.astype(BF)
    value_grad = jnp.einsum("gnl,ngd->ld", probs_b, attention_gradient, preferred_element_type=F32)
    grad_prob = jnp.einsum(
        "ngd,ld->gnl", attention_gradient, value_rows, preferred_element_type=F32
    )
    delta = jnp.transpose(
        jnp.sum(attention_gradient.astype(F32) * attended_rows.astype(F32), axis=-1)
    )
    grad_score = (probs * (grad_prob - delta[..., None]) * SCALE).astype(BF)
    query_grad = jnp.einsum("gnl,ld->ngd", grad_score, keys, preferred_element_type=F32)
    key_grad = jnp.einsum("gnl,ngd->ld", grad_score, query_rows, preferred_element_type=F32)
    return (query_grad, key_grad, value_grad)


def dot(left, right):
    return jnp.dot(left, right, preferred_element_type=F32)


def outer(left, right):
    return lax.dot_general(
        left, right, (((0,), (0,)), ((), ())), preferred_element_type=F32
    )


def back(left, weight):
    return lax.dot_general(
        left, weight, (((1,), (1,)), ((), ())), preferred_element_type=F32
    )


def after(value, *earlier):
    return lax.optimization_barrier((value, *earlier))[0]


def swap(value, mask):
    count = lax.axis_size("shard")
    return lax.ppermute(value, "shard", [(i, i ^ mask) for i in range(count)])


def gather_blocks(value):
    count = lax.axis_size("shard")
    blocks = {0: value}
    bit = count // 2
    while bit:
        for j, block in list(blocks.items()):
            blocks[j ^ bit] = swap(block, bit)
        bit //= 2
    return [blocks[j] for j in range(count)]


def exchange_blocks(pieces):
    return [pieces[0]] + [swap(pieces[j], j) for j in range(1, len(pieces))]


def scatter_blocks(blocks):
    count = len(blocks)
    kept = {j: block for j, block in enumerate(blocks)}
    bit = 1
    while bit < count:
        arrived = {j ^ bit: swap(kept[j].astype(BF), bit) for j in kept if j & bit}
        kept = {j: kept[j] + arrived[j].astype(F32) for j in arrived}
        bit *= 2
    return kept[0]


def assemble(blocks, axis=0):
    shard, count = lax.axis_index("shard"), len(blocks)
    size = blocks[0].shape[axis]
    shape = list(blocks[0].shape)
    shape[axis] = size * count
    whole = jnp.zeros(shape, blocks[0].dtype)
    for j, block in enumerate(blocks):
        whole = lax.dynamic_update_slice_in_dim(whole, block, (shard ^ j) * size, axis)
    return whole


def ring_of(count):
    if count % 2:
        return list(range(count))
    return list(range(0, count, 2)) + list(range(1, count, 2))[::-1]


def ring_steps():
    count = lax.axis_size("rep")
    order = ring_of(count)
    up = [(order[i], order[(i + 1) % count]) for i in range(count)]
    down = [(b, a) for a, b in up]
    place = jnp.asarray([order.index(r) for r in range(count)], jnp.int32)[lax.axis_index("rep")]
    return count, up, down, place


def ring_reduce(up_chunk, down_chunk):
    count, up, down, place = ring_steps()
    one = up_chunk((place - 1) % count).astype(BF)
    two = down_chunk((place + 1) % count).astype(BF)
    for i in range(count - 1):
        one, two = lax.ppermute(one, "rep", up), lax.ppermute(two, "rep", down)
        one = (one.astype(F32) + up_chunk((place - 2 - i) % count)).astype(BF)
        two = (two.astype(F32) + down_chunk((place + 2 + i) % count)).astype(BF)
    return one, two


def ring_gather(one, two):
    count, up, down, place = ring_steps()
    ones, twos = [(place, one)], [(place, two)]
    for i in range(count - 1):
        one, two = lax.ppermute(one, "rep", up), lax.ppermute(two, "rep", down)
        ones.append(((place - 1 - i) % count, one))
        twos.append(((place + 1 + i) % count, two))
    return ones, twos


def place_rows(chunks, whole=None, scale=1, offset=0):
    size = chunks[0][1].shape[0]
    if whole is None:
        whole = jnp.zeros((size * len(chunks) * scale, *chunks[0][1].shape[1:]), F32)
    for index, chunk in chunks:
        whole = lax.dynamic_update_slice_in_dim(
            whole, chunk.astype(F32), (index * scale + offset) * size, 0
        )
    return whole


def local(
    hidden_in,
    out_grad,
    norm1_gain,
    q_weight,
    k_weight,
    v_weight,
    o_weight,
    norm2_gain,
    gate_weight,
    up_weight,
    down_weight,
):
    shard, count = lax.axis_index("shard"), lax.axis_size("shard")
    reps = lax.axis_size("rep")
    tokens, width = hidden_in.shape[1:]
    own_rows = q_weight.shape[0]
    qd, kvd = q_weight.shape[1], k_weight.shape[1]
    heads, kv_heads = qd // HEAD_SIZE, kvd // HEAD_SIZE
    ff = down_weight.shape[0]
    ids = [shard ^ j for j in range(count)]

    gains = assemble(gather_blocks(jnp.stack([norm1_gain, norm2_gain])), 1).astype(F32)
    gain_one, gain_two = gains[0], gains[1]
    kv_blocks = gather_blocks(jnp.concatenate([k_weight, v_weight], axis=1))
    q_blocks = gather_blocks(after(q_weight, kv_blocks[count // 2]))
    w_kv, w_q = assemble(kv_blocks), assemble(q_blocks)

    query_pos = shard * tokens + jnp.arange(tokens, dtype=jnp.int32)
    key_pos = jnp.concatenate([i * tokens + jnp.arange(tokens, dtype=jnp.int32) for i in ids])
    x_full = hidden_in[0].astype(F32)
    inv_one = rms_inverse(x_full)
    normed_one = x_full * inv_one
    first_input = (normed_one * gain_one).astype(BF)
    cosine, sine = rope_tables(query_pos)
    kv_raw = dot(first_input, w_kv)
    keys_own = rotate(kv_raw[:, :kvd].reshape(tokens, kv_heads, HEAD_SIZE), cosine, sine)
    kv_own = jnp.concatenate([keys_own.reshape(tokens, kvd), kv_raw[:, kvd:]], axis=1).astype(BF)
    kv_all = jnp.concatenate(gather_blocks(kv_own), axis=0)
    query_rows = rotate(dot(first_input, w_q).reshape(tokens, heads, HEAD_SIZE), cosine, sine).astype(BF)
    o_blocks = gather_blocks(after(o_weight.T, kv_own, q_blocks[count // 2]))
    w_out = assemble(o_blocks)

    gate_held, up_held = after((gate_weight, up_weight), o_blocks[count // 2])
    pieces = [
        jnp.concatenate(
            [
                lax.dynamic_slice_in_dim(gate_held, i * ff, ff, 1),
                lax.dynamic_slice_in_dim(up_held, i * ff, ff, 1),
            ],
            axis=1,
        )
        for i in ids
    ]
    w_gu = assemble(exchange_blocks(pieces))
    cotangent = out_grad[0]

    query_heads = jnp.transpose(
        query_rows.reshape(tokens, kv_heads, QUERY_PER_KV, HEAD_SIZE), (1, 0, 2, 3)
    )
    total = tokens * count
    key_heads = jnp.transpose(kv_all[:, :kvd].reshape(total, kv_heads, HEAD_SIZE), (1, 0, 2))
    value_heads = jnp.transpose(kv_all[:, kvd:].reshape(total, kv_heads, HEAD_SIZE), (1, 0, 2))
    att_heads, log_total = lax.map(
        partial(head_forward, query_pos=query_pos, key_pos=key_pos),
        (query_heads, key_heads, value_heads),
    )
    attended = jnp.transpose(att_heads, (1, 0, 2, 3)).reshape(tokens, qd).astype(BF)
    x_one = x_full + back(attended, w_out)
    inv_two = rms_inverse(x_one)
    normed_two = x_one * inv_two
    input_two = (normed_two * gain_two).astype(BF)

    h2_all = jnp.concatenate(gather_blocks(input_two), axis=0)
    og_all = jnp.concatenate(gather_blocks(after(cotangent, kv_own)), axis=0)
    gu = dot(h2_all, w_gu)
    gate, upward = gu[:, :ff], gu[:, ff:]
    sigma = jax.nn.sigmoid(gate)
    silu_gate = gate * sigma
    hidden_act = (silu_gate * upward).astype(BF)
    grad_hidden = back(og_all, down_weight)
    grad_gate = (grad_hidden * upward * sigma * (1.0 + gate * (1.0 - sigma))).astype(BF)
    grad_up = (grad_hidden * silu_gate).astype(BF)
    grad_gu = jnp.concatenate([grad_gate, grad_up], axis=1)
    dh2_part = back(grad_gu, w_gu)
    grad_in_two = scatter_blocks(
        [dh2_part[j * tokens : (j + 1) * tokens] for j in range(count)]
    )

    grad_down = outer(hidden_act, og_all)
    half = ff // reps // 2
    down_one, down_two = ring_reduce(
        lambda c: lax.dynamic_slice_in_dim(grad_down, c * 2 * half, half, 0),
        lambda c: lax.dynamic_slice_in_dim(grad_down, c * 2 * half + half, half, 0),
    )
    piece = -(-own_rows // (8 * reps)) * 8
    padded = piece * reps
    h2_padded = jnp.pad(
        h2_all.reshape(total, count, own_rows), ((0, 0), (0, 0), (0, padded - own_rows))
    ).reshape(total, count * padded)
    grad_wgu = outer(h2_padded, grad_gu).reshape(count, padded, 2 * ff)
    share = ring_reduce(
        lambda c: lax.dynamic_slice(grad_wgu, (0, c * piece, 0), (count, piece, ff)),
        lambda c: lax.dynamic_slice(grad_wgu, (0, c * piece, ff), (count, piece, ff)),
    )

    out_part = dot(hidden_act, down_weight)
    output = x_one + scatter_blocks([out_part[j * tokens : (j + 1) * tokens] for j in range(count)])

    grad_gain_two = jnp.sum(grad_in_two * normed_two, axis=0)
    grad_norm_two = grad_in_two * gain_two
    grad_x_one = cotangent.astype(F32) + inv_two * (
        grad_norm_two - normed_two * jnp.mean(grad_norm_two * normed_two, axis=-1, keepdims=True)
    )
    grad_x_one_b = grad_x_one.astype(BF)
    attention_gradient = dot(grad_x_one_b, w_out).astype(BF)
    group = lambda rows: jnp.transpose(
        rows.reshape(tokens, kv_heads, QUERY_PER_KV, HEAD_SIZE), (1, 0, 2, 3)
    )
    q_grad, k_grad, v_grad = lax.map(
        partial(head_backward, query_pos=query_pos, key_pos=key_pos),
        (query_heads, key_heads, value_heads, log_total, group(attention_gradient), group(attended)),
    )
    flat = lambda rows: jnp.transpose(rows, (1, 0, 2)).reshape(total, kvd)
    dkv_part = jnp.concatenate([flat(k_grad), flat(v_grad)], axis=1)
    dkv = scatter_blocks([dkv_part[j * tokens : (j + 1) * tokens] for j in range(count)])
    query_grad = jnp.transpose(q_grad, (1, 0, 2, 3)).reshape(tokens, heads, HEAD_SIZE)
    grad_q = rotate(query_grad, cosine, -sine).reshape(tokens, qd).astype(BF)
    grad_k = rotate(dkv[:, :kvd].reshape(tokens, kv_heads, HEAD_SIZE), cosine, -sine)
    grad_kv = jnp.concatenate([grad_k.reshape(tokens, kvd), dkv[:, kvd:]], axis=1).astype(BF)
    grad_in_one = back(grad_q, w_q) + back(grad_kv, w_kv)
    grad_gain_one = jnp.sum(grad_in_one * normed_one, axis=0)
    grad_norm_one = grad_in_one * gain_one
    grad_input = grad_x_one + inv_one * (
        grad_norm_one - normed_one * jnp.mean(grad_norm_one * normed_one, axis=-1, keepdims=True)
    )

    columns = lambda rows: [
        lax.dynamic_slice_in_dim(rows, i * own_rows, own_rows, 1) for i in ids
    ]
    h1_cols = jnp.concatenate(exchange_blocks(columns(first_input)), axis=0)
    dx_cols = jnp.concatenate(exchange_blocks(columns(grad_x_one_b)), axis=0)
    attended_all = jnp.concatenate(gather_blocks(attended), axis=0)
    dq_all = jnp.concatenate(gather_blocks(grad_q), axis=0)
    dkv_all = jnp.concatenate(gather_blocks(grad_kv), axis=0)
    grad_att = jnp.concatenate(
        [outer(h1_cols, dq_all), outer(h1_cols, dkv_all), outer(dx_cols, attended_all)], axis=1
    )
    half_att = -(-own_rows // (16 * reps)) * 8
    rows_att = half_att * 2 * reps
    grad_att = jnp.pad(grad_att, ((0, rows_att - own_rows), (0, 0)))
    att_one, att_two = ring_reduce(
        lambda c: lax.dynamic_slice_in_dim(grad_att, c * 2 * half_att, half_att, 0),
        lambda c: lax.dynamic_slice_in_dim(grad_att, c * 2 * half_att + half_att, half_att, 0),
    )

    ones, twos = ring_gather(down_one, down_two)
    sum_down = place_rows(twos, place_rows(ones, None, 2, 0), 2, 1)
    gathered = []
    for part in share:
        gathered.append(
            assemble(
                exchange_blocks(
                    [lax.dynamic_index_in_dim(part, i, 0, False) for i in ids]
                ),
                1,
            )
        )
    ones, twos = ring_gather(*gathered)
    sum_gate = place_rows(ones)[:own_rows]
    sum_up = place_rows(twos)[:own_rows]
    ones, twos = ring_gather(att_one, att_two)
    sum_att = place_rows(twos, place_rows(ones, None, 2, 0), 2, 1)[:own_rows]

    both = jnp.stack([grad_gain_one, grad_gain_two])
    pieces = {j: lax.dynamic_slice_in_dim(both, i * own_rows, own_rows, 1) for j, i in enumerate(ids)}
    bit = 1
    while bit < count:
        arrived = {j ^ bit: swap(pieces[j], bit) for j in pieces if j & bit}
        pieces = {j: pieces[j] + arrived[j] for j in arrived}
        bit *= 2
    gain_sum = pieces[0]
    bit = 1
    while bit < reps:
        gain_sum = gain_sum + lax.ppermute(
            gain_sum, "rep", [(i, i ^ bit) for i in range(reps)]
        )
        bit *= 2
    return (
        output[None],
        grad_input[None],
        gain_sum[0],
        sum_att[:, :qd],
        sum_att[:, qd : qd + kvd],
        sum_att[:, qd + kvd : qd + 2 * kvd],
        sum_att[:, qd + 2 * kvd :].T,
        gain_sum[1],
        sum_gate,
        sum_up,
        sum_down,
    )


def solution(mesh):
    placed = (
        P("rep", "shard", None),
        P("rep", "shard", None),
        P("shard"),
        P("shard", None),
        P("shard", None),
        P("shard", None),
        P(None, "shard"),
        P("shard"),
        P("shard", None),
        P("shard", None),
        P("shard", None),
    )
    return jax.shard_map(
        local,
        mesh=mesh,
        in_specs=placed,
        out_specs=(
            P("rep", "shard", None),
            P("rep", "shard", None),
            P("shard"),
            P("shard", None),
            P("shard", None),
            P("shard", None),
            P(None, "shard"),
            P("shard"),
            P("shard", None),
            P("shard", None),
            P("shard", None),
        ),
        check_vma=False,
    )
```

```python
from functools import partial

import jax
import jax.numpy as jnp
from jax import lax
from jax.experimental import pallas as pl
from jax.experimental.pallas import tpu as pltpu
from jax.sharding import PartitionSpec as P

HEAD = 64
PER_KV = 3
EPSILON = 1e-05
SCALE = 0.125
NEGATIVE = -1e30
THETA = 10000.0
BF = jnp.bfloat16
F32 = jnp.float32


def dot(left, right):
    return jnp.dot(left, right, preferred_element_type=F32)


def outer(left, right):
    return lax.dot_general(left, right, (((0,), (0,)), ((), ())), preferred_element_type=F32)


def back(left, weight):
    return lax.dot_general(left, weight, (((1,), (1,)), ((), ())), preferred_element_type=F32)


def after(value, *earlier):
    return lax.optimization_barrier((value, *earlier))[0]


def up_to(size, unit):
    return -(-size // unit) * unit


def swap(value, mask):
    count = lax.axis_size("shard")
    return lax.ppermute(value, "shard", [(i, i ^ mask) for i in range(count)])


def gather_blocks(value):
    count = lax.axis_size("shard")
    blocks = {0: value}
    bit = count // 2
    while bit:
        for j, block in list(blocks.items()):
            blocks[j ^ bit] = swap(block, bit)
        bit //= 2
    return [blocks[j] for j in range(count)]


def exchange_blocks(pieces):
    return [pieces[0]] + [swap(pieces[j], j) for j in range(1, len(pieces))]


def scatter_blocks(blocks):
    count = len(blocks)
    kept = dict(enumerate(blocks))
    bit = 1
    while bit < count:
        arrived = {j ^ bit: swap(kept[j].astype(BF), bit) for j in kept if j & bit}
        kept = {j: kept[j].astype(F32) + arrived[j].astype(F32) for j in arrived}
        bit *= 2
    return kept[0]


def xor_blocks(blocks):
    shard, count = lax.axis_index("shard"), len(blocks)
    bit = 1
    while bit < count:
        odd = (shard & bit) != 0
        blocks = [jnp.where(odd, blocks[j ^ bit], blocks[j]) for j in range(count)]
        bit *= 2
    return blocks


def to_relative(rows, block, padded):
    count = rows.shape[1] // block
    blocks = xor_blocks([rows[:, j * block : (j + 1) * block] for j in range(count)])
    return jnp.concatenate([jnp.pad(b, ((0, 0), (0, padded - block))) for b in blocks], axis=1)


def to_natural(rows, block, padded):
    count = rows.shape[1] // padded
    blocks = xor_blocks([rows[:, j * padded : j * padded + block] for j in range(count)])
    return jnp.concatenate(blocks, axis=1)


def rep_swap(value, bit):
    count = lax.axis_size("rep")
    return lax.ppermute(value, "rep", [(i, i ^ bit) for i in range(count)])


def rep_bits():
    count, bits, bit = lax.axis_size("rep"), [], 1
    while bit < count:
        bits.append(bit)
        bit *= 2
    return bits


def rep_reduce(terms, axis):
    rep = lax.axis_index("rep")
    for bit in rep_bits():
        half = terms.shape[axis] // 2
        low = lax.slice_in_dim(terms, 0, half, axis=axis)
        high = lax.slice_in_dim(terms, half, 2 * half, axis=axis)
        odd = (rep & bit) != 0
        arrived = rep_swap(jnp.where(odd, low, high).astype(BF), bit)
        terms = (jnp.where(odd, high, low).astype(F32) + arrived.astype(F32)).astype(BF)
    return terms


def rep_gather(share, axis):
    rep = lax.axis_index("rep")
    for bit in reversed(rep_bits()):
        arrived = rep_swap(share, bit)
        odd = (rep & bit) != 0
        share = jnp.concatenate(
            [jnp.where(odd, arrived, share), jnp.where(odd, share, arrived)], axis=axis
        )
    return share


def call(body, outs, *args, scalars=(), flops=0):
    smem = [pl.BlockSpec(memory_space=pltpu.SMEM)] * len(scalars)
    vmem = [pl.BlockSpec(memory_space=pltpu.VMEM)] * len(args)
    shapes = [jax.ShapeDtypeStruct(shape, dtype) for shape, dtype in outs]
    moved = sum(a.size * a.dtype.itemsize for a in args)
    moved += sum(s.size * s.dtype.itemsize for s in shapes)
    return pl.pallas_call(
        body,
        out_shape=shapes,
        in_specs=smem + vmem,
        out_specs=[pl.BlockSpec(memory_space=pltpu.VMEM)] * len(outs),
        compiler_params=pltpu.CompilerParams(vmem_limit_bytes=56 * 2**20),
        cost_estimate=pl.CostEstimate(flops=flops, bytes_accessed=moved, transcendentals=0),
    )(*scalars, *args)


def turn(head, cosine, sine):
    half = HEAD // 2
    swapped = jnp.concatenate([head[:, half:], head[:, :half]], axis=1)
    return head * cosine + swapped * sine


def normed(rows, width):
    inverse = lax.rsqrt(jnp.sum(rows * rows, axis=-1, keepdims=True) / width + EPSILON)
    return rows * inverse, inverse


def kv_body(width, x_ref, gain_ref, cos_ref, sin_ref, *refs):
    weights, (h_ref, kv_ref) = refs[:-2], refs[-2:]
    block = weights[0].shape[0]
    padded = x_ref.shape[1] // len(weights)
    rows, _ = normed(x_ref[...].astype(F32), width)
    h_ref[...] = (rows * gain_ref[...]).astype(BF)
    total = None
    for j, weight in enumerate(weights):
        term = dot(h_ref[:, j * padded : j * padded + block], weight[...])
        total = term if total is None else total + term
    kvd = total.shape[1] // 2
    for h in range(kvd // HEAD):
        head = total[:, h * HEAD : (h + 1) * HEAD]
        kv_ref[:, h * HEAD : (h + 1) * HEAD] = turn(head, cos_ref[...], sin_ref[...]).astype(BF)
    kv_ref[:, kvd:] = total[:, kvd:].astype(BF)


def allowed_keys(shard, tokens, total, rows):
    key = lax.broadcasted_iota(jnp.int32, (rows, total), 1)
    query = lax.broadcasted_iota(jnp.int32, (rows, total), 0)
    owner = (key // tokens) ^ shard
    return owner * tokens + key % tokens <= shard * tokens + query % tokens


def stacked(rows, group):
    first = group * PER_KV
    return jnp.concatenate(
        [rows[:, h * HEAD : (h + 1) * HEAD] for h in range(first, first + PER_KV)], axis=0
    )


def probabilities(query, key, allowed):
    scores = jnp.where(allowed, back(query, key) * SCALE, NEGATIVE)
    weights = jnp.exp(scores - jnp.max(scores, axis=-1, keepdims=True))
    return weights / jnp.sum(weights, axis=-1, keepdims=True)


def attend_body(count, shard_ref, h_ref, cos_ref, sin_ref, *refs):
    weights, kvs = refs[:count], refs[count : 2 * count]
    query_ref, attended_ref = refs[2 * count :]
    tokens, block = h_ref.shape[0], weights[0].shape[0]
    padded = h_ref.shape[1] // count
    kvd = kvs[0].shape[1] // 2
    total = None
    for j, weight in enumerate(weights):
        term = dot(h_ref[:, j * padded : j * padded + block], weight[...])
        total = term if total is None else total + term
    for h in range(total.shape[1] // HEAD):
        head = total[:, h * HEAD : (h + 1) * HEAD]
        query_ref[:, h * HEAD : (h + 1) * HEAD] = turn(head, cos_ref[...], sin_ref[...]).astype(BF)
    allowed = allowed_keys(shard_ref[0], tokens, tokens * count, tokens * PER_KV)
    for g in range(kvd // HEAD):
        low = g * HEAD
        key = jnp.concatenate([kv[:, low : low + HEAD] for kv in kvs], axis=0)
        value = jnp.concatenate([kv[:, kvd + low : kvd + low + HEAD] for kv in kvs], axis=0)
        prob = probabilities(stacked(query_ref, g), key, allowed)
        rows = dot(prob.astype(BF), value).astype(BF)
        for k in range(PER_KV):
            h = g * PER_KV + k
            attended_ref[:, h * HEAD : (h + 1) * HEAD] = rows[k * tokens : (k + 1) * tokens]


def residual_body(width, attended_ref, x_ref, gain_ref, *refs):
    weights, (one_ref, h_ref) = refs[:-2], refs[-2:]
    block = weights[0].shape[0]
    padded = x_ref.shape[1] // len(weights)
    one_ref[...] = x_ref[...].astype(F32)
    for j, weight in enumerate(weights):
        one_ref[:, j * padded : j * padded + block] += back(attended_ref[...], weight[...])
    rows, _ = normed(one_ref[...], width)
    h_ref[...] = (rows * gain_ref[...]).astype(BF)


def norm_back(grad, rows, inverse, gain, width):
    scaled = grad * gain
    return inverse * (scaled - rows * (jnp.sum(scaled * rows, axis=-1, keepdims=True) / width))


def residual_back_body(width, grad_ref, one_ref, cot_ref, gain_ref, *refs):
    weights, (dx_ref, dxb_ref, gain_grad_ref, datt_ref) = refs[:-4], refs[-4:]
    block = weights[0].shape[0]
    padded = one_ref.shape[1] // len(weights)
    rows, inverse = normed(one_ref[...], width)
    grad = grad_ref[...]
    gain_grad_ref[...] = jnp.sum(grad * rows, axis=0, keepdims=True)
    dx_ref[...] = cot_ref[...].astype(F32) + norm_back(grad, rows, inverse, gain_ref[...], width)
    dxb_ref[...] = dx_ref[...].astype(BF)
    total = None
    for j, weight in enumerate(weights):
        term = dot(dxb_ref[:, j * padded : j * padded + block], weight[...])
        total = term if total is None else total + term
    datt_ref[...] = total.astype(BF)


def attend_back_body(count, shard_ref, query_ref, att_ref, datt_ref, cos_ref, sin_ref, *refs):
    kvs, (dq_ref, dkv_ref) = refs[:count], refs[count:]
    tokens = query_ref.shape[0]
    kvd = kvs[0].shape[1] // 2
    allowed = allowed_keys(shard_ref[0], tokens, tokens * count, tokens * PER_KV)
    for g in range(kvd // HEAD):
        low = g * HEAD
        key = jnp.concatenate([kv[:, low : low + HEAD] for kv in kvs], axis=0)
        value = jnp.concatenate([kv[:, kvd + low : kvd + low + HEAD] for kv in kvs], axis=0)
        query, datt = stacked(query_ref, g), stacked(datt_ref, g)
        att = stacked(att_ref, g)
        prob = probabilities(query, key, allowed)
        dkv_ref[:, kvd + low : kvd + low + HEAD] = outer(prob.astype(BF), datt).astype(BF)
        delta = jnp.sum(datt.astype(F32) * att.astype(F32), axis=-1, keepdims=True)
        dscore = (prob * (back(datt, value) - delta) * SCALE).astype(BF)
        dkv_ref[:, low : low + HEAD] = outer(dscore, query).astype(BF)
        rows = dot(dscore, key)
        for k in range(PER_KV):
            h = g * PER_KV + k
            head = rows[k * tokens : (k + 1) * tokens]
            dq_ref[:, h * HEAD : (h + 1) * HEAD] = turn(head, cos_ref[...], -sin_ref[...]).astype(BF)


def turn_keys_body(dkv_ref, cos_ref, sin_ref, out_ref):
    kvd = dkv_ref.shape[1] // 2
    for h in range(kvd // HEAD):
        head = dkv_ref[:, h * HEAD : (h + 1) * HEAD]
        out_ref[:, h * HEAD : (h + 1) * HEAD] = turn(head, cos_ref[...], -sin_ref[...]).astype(BF)
    out_ref[:, kvd:] = dkv_ref[:, kvd:].astype(BF)


def input_back_body(width, count, dq_ref, dkv_ref, x_ref, dx_ref, gain_ref, *refs):
    wqs, wkvs = refs[:count], refs[count : 2 * count]
    out_ref, gain_grad_ref, grad_ref = refs[2 * count :]
    block = wqs[0].shape[0]
    padded = x_ref.shape[1] // count
    grad_ref[...] = jnp.zeros_like(grad_ref)
    for j in range(count):
        grad_ref[:, j * padded : j * padded + block] = back(dq_ref[...], wqs[j][...]) + back(
            dkv_ref[...], wkvs[j][...]
        )
    rows, inverse = normed(x_ref[...].astype(F32), width)
    grad = grad_ref[...]
    gain_grad_ref[...] = jnp.sum(grad * rows, axis=0, keepdims=True)
    out_ref[...] = dx_ref[...] + norm_back(grad, rows, inverse, gain_ref[...], width)


def local(
    hidden_in,
    out_grad,
    norm1_gain,
    q_weight,
    k_weight,
    v_weight,
    o_weight,
    norm2_gain,
    gate_weight,
    up_weight,
    down_weight,
):
    shard, count = lax.axis_index("shard"), lax.axis_size("shard")
    reps = lax.axis_size("rep")
    tokens, width = hidden_in.shape[1:]
    block = q_weight.shape[0]
    padded = up_to(block, 128)
    wide = count * padded
    qd, kvd = q_weight.shape[1], k_weight.shape[1]
    ff = down_weight.shape[0]
    total = tokens * count
    far = count // 2
    here = shard.astype(jnp.int32)[None]

    kv_blocks = gather_blocks(jnp.concatenate([k_weight, v_weight], axis=1))
    gains = gather_blocks(jnp.pad(jnp.stack([norm1_gain, norm2_gain]), ((0, 0), (0, padded - block))))
    gains = jnp.concatenate(gains, axis=1).astype(F32)
    gain_one, gain_two = gains[:1], gains[1:]
    q_blocks = gather_blocks(after(q_weight, kv_blocks[far]))

    positions = (shard * tokens + jnp.arange(tokens, dtype=jnp.int32)).astype(F32)
    freqs = THETA ** (-(jnp.arange(HEAD // 2, dtype=F32) * 2.0 / HEAD))
    angles = positions[:, None] * freqs[None, :]
    cosine, sine = jnp.cos(angles), jnp.sin(angles)
    cosine = jnp.concatenate([cosine, cosine], axis=1)
    sine = jnp.concatenate([-sine, sine], axis=1)

    x_rel = to_relative(hidden_in[0], block, padded)
    cot_rel = to_relative(out_grad[0], block, padded)
    first_input, kv_own = call(
        partial(kv_body, width),
        [((tokens, wide), BF), ((tokens, 2 * kvd), BF)],
        x_rel, gain_one, cosine, sine, *kv_blocks,
        flops=4 * tokens * width * kvd,
    )
    kv_all = gather_blocks(kv_own)
    o_blocks = gather_blocks(after(o_weight.T, kv_own, q_blocks[far]))
    query, attended = call(
        partial(attend_body, count),
        [((tokens, qd), BF), ((tokens, qd), BF)],
        first_input, cosine, sine, *q_blocks, *kv_all,
        scalars=(here,),
        flops=2 * tokens * qd * (width + 2 * total),
    )
    x_one, input_two = call(
        partial(residual_body, width),
        [((tokens, wide), F32), ((tokens, wide), BF)],
        attended, x_rel, gain_two, *o_blocks,
        flops=2 * tokens * qd * width,
    )

    gate_held, up_held, _ = lax.optimization_barrier((gate_weight, up_weight, o_blocks[far]))
    split = lambda rows: xor_blocks([rows[:, j * ff : (j + 1) * ff] for j in range(count)])
    pieces = [
        jnp.concatenate(pair, axis=1) for pair in zip(split(gate_held), split(up_held), strict=True)
    ]
    w_gu = jnp.concatenate(
        [jnp.pad(b, ((0, padded - block), (0, 0))) for b in exchange_blocks(pieces)], axis=0
    )
    og_all = jnp.concatenate(gather_blocks(after(out_grad[0], kv_own)), axis=0)

    reorder = lambda rows, j: jnp.concatenate(
        [rows[:, (i ^ j) * padded : ((i ^ j) + 1) * padded] for i in range(count)], axis=1
    )
    h2_all = jnp.concatenate(
        [reorder(rows, j) for j, rows in enumerate(gather_blocks(input_two))], axis=0
    )
    grad_hidden = back(og_all, down_weight)
    gu = dot(h2_all, w_gu)
    gate, upward = gu[:, :ff], gu[:, ff:]
    sigma = jax.nn.sigmoid(gate)
    silu_gate = gate * sigma
    hidden_act = (silu_gate * upward).astype(BF)
    grad_gate = (grad_hidden * upward * sigma * (1.0 + gate * (1.0 - sigma))).astype(BF)
    grad_up = (grad_hidden * silu_gate).astype(BF)
    grad_gu = jnp.concatenate([grad_gate, grad_up], axis=1)
    dh2_part = back(grad_gu, w_gu).astype(BF)
    grad_in_two = scatter_blocks(
        [reorder(dh2_part[j * tokens : (j + 1) * tokens], j) for j in range(count)]
    )

    down_share = rep_reduce(outer(hidden_act, og_all), 0)
    rows_gu = up_to(block, 8 * reps)
    fit = lambda grad: jnp.pad(
        grad.reshape(count, padded, ff)[:, :rows_gu], ((0, 0), (0, max(rows_gu - padded, 0)), (0, 0))
    )
    gate_share = rep_reduce(fit(outer(h2_all, grad_gate)), 1)
    up_share = rep_reduce(fit(outer(h2_all, grad_up)), 1)

    out_part = dot(hidden_act, down_weight)
    out_sum = scatter_blocks([out_part[j * tokens : (j + 1) * tokens] for j in range(count)])
    output = to_natural(x_one, block, padded) + out_sum

    grad_x_one, grad_x_one_b, gain_two_grad, grad_attended = call(
        partial(residual_back_body, width),
        [((tokens, wide), F32), ((tokens, wide), BF), ((1, wide), F32), ((tokens, qd), BF)],
        grad_in_two, x_one, cot_rel, gain_two, *o_blocks,
        flops=2 * tokens * qd * width,
    )
    grad_q, dkv_part = call(
        partial(attend_back_body, count),
        [((tokens, qd), BF), ((total, 2 * kvd), BF)],
        query, attended, grad_attended, cosine, sine, *kv_all,
        scalars=(here,),
        flops=10 * tokens * qd * total,
    )
    dkv = scatter_blocks([dkv_part[j * tokens : (j + 1) * tokens] for j in range(count)])
    (grad_kv,) = call(turn_keys_body, [((tokens, 2 * kvd), BF)], dkv, cosine, sine)

    columns = lambda rows: [rows[:, j * padded : j * padded + block] for j in range(count)]
    h1_cols = jnp.concatenate(exchange_blocks(columns(first_input)), axis=0)
    attended_all = jnp.concatenate(gather_blocks(attended), axis=0)
    dx_cols = jnp.concatenate(exchange_blocks(columns(grad_x_one_b)), axis=0)
    rows_att = up_to(block, 8 * reps)
    pad_rows = lambda grad: jnp.pad(grad, ((0, rows_att - block), (0, 0)))
    out_share = rep_reduce(pad_rows(outer(dx_cols, attended_all)), 0)
    dq_all = jnp.concatenate(gather_blocks(grad_q), axis=0)
    dkv_all = jnp.concatenate(gather_blocks(grad_kv), axis=0)
    qkv_share = rep_reduce(
        pad_rows(jnp.concatenate([outer(h1_cols, dq_all), outer(h1_cols, dkv_all)], axis=1)), 0
    )
    grad_input, gain_one_grad, _ = call(
        partial(input_back_body, width, count),
        [((tokens, wide), F32), ((1, wide), F32), ((tokens, wide), F32)],
        grad_q, grad_kv, x_rel, grad_x_one, gain_one, *q_blocks, *kv_blocks,
        flops=2 * tokens * width * (qd + 2 * kvd),
    )
    grad_input = to_natural(grad_input, block, padded)

    sum_down = rep_gather(down_share, 0).astype(F32)
    arrived = [
        exchange_blocks([share[j] for j in range(count)]) for share in (gate_share, up_share)
    ]
    sum_gate, sum_up = [
        rep_gather(jnp.concatenate(xor_blocks(blocks), axis=1), 0)[:block].astype(F32)
        for blocks in arrived
    ]
    sum_out = rep_gather(out_share, 0)[:block].astype(F32).T
    sum_qkv = rep_gather(qkv_share, 0)[:block].astype(F32)

    both = jnp.concatenate([gain_one_grad, gain_two_grad], axis=0)
    kept = {j: both[:, j * padded : j * padded + block] for j in range(count)}
    bit = 1
    while bit < count:
        arrived = {j ^ bit: swap(kept[j], bit) for j in kept if j & bit}
        kept = {j: kept[j] + arrived[j] for j in arrived}
        bit *= 2
    gain_sum = kept[0]
    for bit in rep_bits():
        gain_sum = gain_sum + rep_swap(gain_sum, bit)
    return (
        output[None],
        grad_input[None],
        gain_sum[0],
        sum_qkv[:, :qd],
        sum_qkv[:, qd : qd + kvd],
        sum_qkv[:, qd + kvd :],
        sum_out,
        gain_sum[1],
        sum_gate,
        sum_up,
        sum_down,
    )


def solution(mesh):
    placed = (
        P("rep", "shard", None),
        P("rep", "shard", None),
        P("shard"),
        P("shard", None),
        P("shard", None),
        P("shard", None),
        P(None, "shard"),
        P("shard"),
        P("shard", None),
        P("shard", None),
        P("shard", None),
    )
    return jax.shard_map(
        local,
        mesh=mesh,
        in_specs=placed,
        out_specs=(
            P("rep", "shard", None),
            P("rep", "shard", None),
            P("shard"),
            P("shard", None),
            P("shard", None),
            P("shard", None),
            P(None, "shard"),
            P("shard"),
            P("shard", None),
            P("shard", None),
            P("shard", None),
        ),
        check_vma=False,
    )
```

```python
from functools import partial

import jax
import jax.numpy as jnp
from jax import lax
from jax.experimental import pallas as pl
from jax.experimental.pallas import tpu as pltpu
from jax.sharding import PartitionSpec as P

HEAD = 64
PER_KV = 3
EPSILON = 1e-05
SCALE = 0.125
NEGATIVE = -1e30
THETA = 10000.0
BF = jnp.bfloat16
F32 = jnp.float32


def dot(left, right):
    return jnp.dot(left, right, preferred_element_type=F32)


def outer(left, right):
    return lax.dot_general(left, right, (((0,), (0,)), ((), ())), preferred_element_type=F32)


def back(left, weight):
    return lax.dot_general(left, weight, (((1,), (1,)), ((), ())), preferred_element_type=F32)


def after(value, *earlier):
    return lax.optimization_barrier((value, *earlier))[0]


def up_to(size, unit):
    return -(-size // unit) * unit


def swap(value, mask):
    count = lax.axis_size("shard")
    return lax.ppermute(value, "shard", [(i, i ^ mask) for i in range(count)])


def gather_blocks(value):
    count = lax.axis_size("shard")
    blocks = {0: value}
    bit = count // 2
    while bit:
        for j, block in list(blocks.items()):
            blocks[j ^ bit] = swap(block, bit)
        bit //= 2
    return [blocks[j] for j in range(count)]


def exchange_blocks(pieces):
    return [pieces[0]] + [swap(pieces[j], j) for j in range(1, len(pieces))]


def scatter_blocks(blocks):
    count = len(blocks)
    kept = dict(enumerate(blocks))
    bit = 1
    while bit < count:
        sent = {j: kept[j].astype(BF) for j in kept if j & bit}
        arrived = {j ^ bit: swap(block, bit) for j, block in sent.items()}
        kept = {j: kept[j].astype(F32) + arrived[j].astype(F32) for j in arrived}
        bit *= 2
    return kept[0], sent[count // 2]


def xor_blocks(blocks):
    shard, count = lax.axis_index("shard"), len(blocks)
    bit = 1
    while bit < count:
        odd = (shard & bit) != 0
        blocks = [jnp.where(odd, blocks[j ^ bit], blocks[j]) for j in range(count)]
        bit *= 2
    return blocks


def to_relative(rows, block, padded):
    count = rows.shape[1] // block
    blocks = xor_blocks([rows[:, j * block : (j + 1) * block] for j in range(count)])
    return jnp.concatenate([jnp.pad(b, ((0, 0), (0, padded - block))) for b in blocks], axis=1)


def to_natural(rows, block, padded):
    count = rows.shape[1] // padded
    blocks = xor_blocks([rows[:, j * padded : j * padded + block] for j in range(count)])
    return jnp.concatenate(blocks, axis=1)


def rep_swap(value, bit):
    count = lax.axis_size("rep")
    return lax.ppermute(value, "rep", [(i, i ^ bit) for i in range(count)])


def exchange_pairs(pairs):
    count, rep = len(pairs), lax.axis_index("rep")
    far = count // 2
    if len(rep_bits()) < 2:
        return list(zip(*[exchange_blocks(list(p)) for p in zip(*pairs, strict=True)], strict=True))
    second, fourth = (rep & 1) != 0, (rep & 2) != 0
    half = pairs[0][0].shape[0] // 2
    quarters = [jnp.where(second, two, one) for one, two in pairs[far:]]
    quarters = [jnp.where(fourth, q[half:], q[:half]) for q in quarters]
    near = [pairs[0]] + [tuple(swap(p, j) for p in pairs[j]) for j in range(1, far)]
    mine = jnp.stack([swap(q, far + k) for k, q in enumerate(quarters)])
    theirs = rep_swap(mine, 2)
    mine = jnp.concatenate(
        [jnp.where(fourth, theirs, mine), jnp.where(fourth, mine, theirs)], axis=1
    )
    theirs = rep_swap(mine, 1)
    ones, twos = jnp.where(second, theirs, mine), jnp.where(second, mine, theirs)
    return near + [(ones[k], twos[k]) for k in range(far)]


def rep_bits():
    count, bits, bit = lax.axis_size("rep"), [], 1
    while bit < count:
        bits.append(bit)
        bit *= 2
    return bits


def turned(bits, first):
    return bits[first : first + 1] + bits[:first] + bits[first + 1 :]


def rep_reduce(terms, axis, first=0, gates=()):
    rep = lax.axis_index("rep")
    for step, bit in enumerate(turned(rep_bits(), first)):
        half = terms.shape[axis] // 2
        low = lax.slice_in_dim(terms, 0, half, axis=axis)
        high = lax.slice_in_dim(terms, half, 2 * half, axis=axis)
        odd = (rep & bit) != 0
        arrived = rep_swap(jnp.where(odd, low, high).astype(BF), bit)
        if step < len(gates):
            arrived = after(arrived, gates[step])
        terms = (jnp.where(odd, high, low).astype(F32) + arrived.astype(F32)).astype(BF)
    return terms


def rep_gather(share, axis, first=0):
    rep = lax.axis_index("rep")
    for bit in reversed(turned(rep_bits(), first)):
        arrived = rep_swap(share, bit)
        odd = (rep & bit) != 0
        share = jnp.concatenate(
            [jnp.where(odd, arrived, share), jnp.where(odd, share, arrived)], axis=axis
        )
    return share


def call(body, outs, *args, scalars=(), flops=0):
    smem = [pl.BlockSpec(memory_space=pltpu.SMEM)] * len(scalars)
    vmem = [pl.BlockSpec(memory_space=pltpu.VMEM)] * len(args)
    shapes = [jax.ShapeDtypeStruct(shape, dtype) for shape, dtype in outs]
    moved = sum(a.size * a.dtype.itemsize for a in args)
    moved += sum(s.size * s.dtype.itemsize for s in shapes)
    return pl.pallas_call(
        body,
        out_shape=shapes,
        in_specs=smem + vmem,
        out_specs=[pl.BlockSpec(memory_space=pltpu.VMEM)] * len(outs),
        compiler_params=pltpu.CompilerParams(vmem_limit_bytes=56 * 2**20),
        cost_estimate=pl.CostEstimate(flops=flops, bytes_accessed=moved, transcendentals=0),
    )(*scalars, *args)


def turn(head, cosine, sine):
    half = HEAD // 2
    swapped = jnp.concatenate([head[:, half:], head[:, :half]], axis=1)
    return head * cosine + swapped * sine


def normed(rows, width):
    inverse = lax.rsqrt(jnp.sum(rows * rows, axis=-1, keepdims=True) / width + EPSILON)
    return rows * inverse, inverse


def kv_body(width, x_ref, gain_ref, cos_ref, sin_ref, *refs):
    weights, (h_ref, kv_ref) = refs[:-2], refs[-2:]
    block = weights[0].shape[0]
    padded = x_ref.shape[1] // len(weights)
    rows, _ = normed(x_ref[...].astype(F32), width)
    h_ref[...] = (rows * gain_ref[...]).astype(BF)
    total = None
    for j, weight in enumerate(weights):
        term = dot(h_ref[:, j * padded : j * padded + block], weight[...])
        total = term if total is None else total + term
    kvd = total.shape[1] // 2
    for h in range(kvd // HEAD):
        head = total[:, h * HEAD : (h + 1) * HEAD]
        kv_ref[:, h * HEAD : (h + 1) * HEAD] = turn(head, cos_ref[...], sin_ref[...]).astype(BF)
    kv_ref[:, kvd:] = total[:, kvd:].astype(BF)


def allowed_keys(shard, tokens, total, rows):
    key = lax.broadcasted_iota(jnp.int32, (rows, total), 1)
    query = lax.broadcasted_iota(jnp.int32, (rows, total), 0)
    owner = (key // tokens) ^ shard
    return owner * tokens + key % tokens <= shard * tokens + query % tokens


def stacked(rows, group):
    first = group * PER_KV
    return jnp.concatenate(
        [rows[:, h * HEAD : (h + 1) * HEAD] for h in range(first, first + PER_KV)], axis=0
    )


def probabilities(query, key, allowed):
    scores = jnp.where(allowed, back(query * SCALE, key), NEGATIVE)
    weights = jnp.exp(scores - jnp.max(scores, axis=-1, keepdims=True))
    return weights * (1.0 / jnp.sum(weights, axis=-1, keepdims=True))


def arrange_body(*refs):
    blocks, out_ref = refs[:-1], refs[-1]
    count, (tokens, wide) = len(blocks), blocks[0].shape
    padded = wide // count
    for j, rows in enumerate(blocks):
        for i in range(count):
            out_ref[j * tokens : (j + 1) * tokens, i * padded : (i + 1) * padded] = rows[
                :, (i ^ j) * padded : ((i ^ j) + 1) * padded
            ]


def attend_body(count, shard_ref, h_ref, cos_ref, sin_ref, *refs):
    weights, kvs = refs[:count], refs[count : 2 * count]
    query_ref, attended_ref = refs[2 * count :]
    tokens, block = h_ref.shape[0], weights[0].shape[0]
    padded = h_ref.shape[1] // count
    kvd = kvs[0].shape[1] // 2
    total = None
    for j, weight in enumerate(weights):
        term = dot(h_ref[:, j * padded : j * padded + block], weight[...])
        total = term if total is None else total + term
    for h in range(total.shape[1] // HEAD):
        head = total[:, h * HEAD : (h + 1) * HEAD]
        query_ref[:, h * HEAD : (h + 1) * HEAD] = turn(head, cos_ref[...], sin_ref[...]).astype(BF)
    allowed = allowed_keys(shard_ref[0], tokens, tokens * count, tokens * PER_KV)
    for g in range(kvd // HEAD):
        low = g * HEAD
        key = jnp.concatenate([kv[:, low : low + HEAD] for kv in kvs], axis=0)
        value = jnp.concatenate([kv[:, kvd + low : kvd + low + HEAD] for kv in kvs], axis=0)
        prob = probabilities(stacked(query_ref, g), key, allowed)
        rows = dot(prob.astype(BF), value).astype(BF)
        for k in range(PER_KV):
            h = g * PER_KV + k
            attended_ref[:, h * HEAD : (h + 1) * HEAD] = rows[k * tokens : (k + 1) * tokens]


def residual_body(width, attended_ref, x_ref, gain_ref, *refs):
    weights, (one_ref, h_ref) = refs[:-2], refs[-2:]
    block = weights[0].shape[0]
    padded = x_ref.shape[1] // len(weights)
    one_ref[...] = x_ref[...].astype(F32)
    for j, weight in enumerate(weights):
        one_ref[:, j * padded : j * padded + block] += back(attended_ref[...], weight[...])
    rows, _ = normed(one_ref[...], width)
    h_ref[...] = (rows * gain_ref[...]).astype(BF)


def norm_back(grad, rows, inverse, gain, width):
    scaled = grad * gain
    return inverse * (scaled - rows * (jnp.sum(scaled * rows, axis=-1, keepdims=True) / width))


def residual_back_body(width, grad_ref, one_ref, cot_ref, gain_ref, *refs):
    weights, (dx_ref, dxb_ref, gain_grad_ref, datt_ref) = refs[:-4], refs[-4:]
    block = weights[0].shape[0]
    padded = one_ref.shape[1] // len(weights)
    rows, inverse = normed(one_ref[...], width)
    grad = grad_ref[...]
    gain_grad_ref[...] = jnp.sum(grad * rows, axis=0, keepdims=True)
    dx_ref[...] = cot_ref[...].astype(F32) + norm_back(grad, rows, inverse, gain_ref[...], width)
    dxb_ref[...] = dx_ref[...].astype(BF)
    total = None
    for j, weight in enumerate(weights):
        term = dot(dxb_ref[:, j * padded : j * padded + block], weight[...])
        total = term if total is None else total + term
    datt_ref[...] = total.astype(BF)


def attend_back_body(count, shard_ref, query_ref, att_ref, datt_ref, cos_ref, sin_ref, *refs):
    kvs, (dq_ref, dkv_ref) = refs[:count], refs[count:]
    tokens = query_ref.shape[0]
    kvd = kvs[0].shape[1] // 2
    allowed = allowed_keys(shard_ref[0], tokens, tokens * count, tokens * PER_KV)
    for g in range(kvd // HEAD):
        low = g * HEAD
        key = jnp.concatenate([kv[:, low : low + HEAD] for kv in kvs], axis=0)
        value = jnp.concatenate([kv[:, kvd + low : kvd + low + HEAD] for kv in kvs], axis=0)
        query, datt = stacked(query_ref, g), stacked(datt_ref, g)
        att = stacked(att_ref, g)
        prob = probabilities(query, key, allowed)
        dkv_ref[:, kvd + low : kvd + low + HEAD] = outer(prob.astype(BF), datt).astype(BF)
        delta = jnp.sum(datt.astype(F32) * att.astype(F32), axis=-1, keepdims=True)
        dscore = (prob * (back(datt, value) - delta) * SCALE).astype(BF)
        dkv_ref[:, low : low + HEAD] = outer(dscore, query).astype(BF)
        rows = dot(dscore, key)
        for k in range(PER_KV):
            h = g * PER_KV + k
            head = rows[k * tokens : (k + 1) * tokens]
            dq_ref[:, h * HEAD : (h + 1) * HEAD] = turn(head, cos_ref[...], -sin_ref[...]).astype(BF)


def turn_keys_body(dkv_ref, cos_ref, sin_ref, out_ref):
    kvd = dkv_ref.shape[1] // 2
    for h in range(kvd // HEAD):
        head = dkv_ref[:, h * HEAD : (h + 1) * HEAD]
        out_ref[:, h * HEAD : (h + 1) * HEAD] = turn(head, cos_ref[...], -sin_ref[...]).astype(BF)
    out_ref[:, kvd:] = dkv_ref[:, kvd:].astype(BF)


def input_back_body(width, count, dq_ref, dkv_ref, x_ref, dx_ref, gain_ref, *refs):
    wqs, wkvs = refs[:count], refs[count : 2 * count]
    out_ref, gain_grad_ref, grad_ref = refs[2 * count :]
    block = wqs[0].shape[0]
    padded = x_ref.shape[1] // count
    grad_ref[...] = jnp.zeros_like(grad_ref)
    for j in range(count):
        grad_ref[:, j * padded : j * padded + block] = back(dq_ref[...], wqs[j][...]) + back(
            dkv_ref[...], wkvs[j][...]
        )
    rows, inverse = normed(x_ref[...].astype(F32), width)
    grad = grad_ref[...]
    gain_grad_ref[...] = jnp.sum(grad * rows, axis=0, keepdims=True)
    out_ref[...] = dx_ref[...] + norm_back(grad, rows, inverse, gain_ref[...], width)


def local(
    hidden_in,
    out_grad,
    norm1_gain,
    q_weight,
    k_weight,
    v_weight,
    o_weight,
    norm2_gain,
    gate_weight,
    up_weight,
    down_weight,
):
    shard, count = lax.axis_index("shard"), lax.axis_size("shard")
    reps = lax.axis_size("rep")
    tokens, width = hidden_in.shape[1:]
    block = q_weight.shape[0]
    padded = up_to(block, 128)
    wide = count * padded
    qd, kvd = q_weight.shape[1], k_weight.shape[1]
    ff = down_weight.shape[0]
    total = tokens * count
    far = count // 2
    here = shard.astype(jnp.int32)[None]

    kv_blocks = gather_blocks(jnp.concatenate([k_weight, v_weight], axis=1))
    gains = gather_blocks(jnp.pad(jnp.stack([norm1_gain, norm2_gain]), ((0, 0), (0, padded - block))))
    gains = jnp.concatenate(gains, axis=1).astype(F32)
    gain_one, gain_two = gains[:1], gains[1:]
    q_blocks = gather_blocks(after(q_weight, kv_blocks[far]))

    positions = (shard * tokens + jnp.arange(tokens, dtype=jnp.int32)).astype(F32)
    freqs = THETA ** (-(jnp.arange(HEAD // 2, dtype=F32) * 2.0 / HEAD))
    angles = positions[:, None] * freqs[None, :]
    cosine, sine = jnp.cos(angles), jnp.sin(angles)
    cosine = jnp.concatenate([cosine, cosine], axis=1)
    sine = jnp.concatenate([-sine, sine], axis=1)

    x_rel = to_relative(hidden_in[0], block, padded)
    cot_rel = to_relative(out_grad[0], block, padded)
    first_input, kv_own = call(
        partial(kv_body, width),
        [((tokens, wide), BF), ((tokens, 2 * kvd), BF)],
        x_rel, gain_one, cosine, sine, *kv_blocks,
        flops=4 * tokens * width * kvd,
    )
    kv_all = gather_blocks(kv_own)
    o_held, gate_held, up_held = lax.optimization_barrier(
        (o_weight.T, gate_weight, up_weight, q_blocks[far], kv_all[far])
    )[:3]
    o_blocks = gather_blocks(o_held)
    split = lambda rows: xor_blocks([rows[:, j * ff : (j + 1) * ff] for j in range(count)])
    gate_blocks, up_blocks = zip(
        *exchange_pairs(list(zip(split(gate_held), split(up_held), strict=True))), strict=True
    )
    query, attended = call(
        partial(attend_body, count),
        [((tokens, qd), BF), ((tokens, qd), BF)],
        first_input, cosine, sine, *q_blocks, *kv_all,
        scalars=(here,),
        flops=2 * tokens * qd * (width + 2 * total),
    )
    x_one, input_two = call(
        partial(residual_body, width),
        [((tokens, wide), F32), ((tokens, wide), BF)],
        attended, x_rel, gain_two, *o_blocks,
        flops=2 * tokens * qd * width,
    )

    joined = lambda blocks: jnp.concatenate(
        [jnp.pad(b, ((0, padded - block), (0, 0))) for b in blocks], axis=0
    )
    w_gate, w_up = joined(gate_blocks), joined(up_blocks)
    og_all = jnp.concatenate(gather_blocks(after(out_grad[0], o_blocks[far])), axis=0)

    reorder = lambda rows, j: jnp.concatenate(
        [rows[:, (i ^ j) * padded : ((i ^ j) + 1) * padded] for i in range(count)], axis=1
    )
    h2_blocks = gather_blocks(input_two)
    (h2_all,) = call(arrange_body, [((total, wide), BF)], *h2_blocks)
    grad_hidden = back(og_all, down_weight)
    gate, upward = dot(h2_all, w_gate), dot(h2_all, w_up)
    sigma = jax.nn.sigmoid(gate)
    silu_gate = gate * sigma
    hidden_act = (silu_gate * upward).astype(BF)
    grad_gate = (grad_hidden * upward * sigma * (1.0 + gate * (1.0 - sigma))).astype(BF)
    grad_up = (grad_hidden * silu_gate).astype(BF)
    dh2_part = (back(grad_gate, w_gate) + back(grad_up, w_up)).astype(BF)
    grad_in_two, _ = scatter_blocks(
        [reorder(dh2_part[j * tokens : (j + 1) * tokens], j) for j in range(count)]
    )
    grad_down = outer(hidden_act, og_all)
    rows_gu = up_to(block, 8 * reps)
    fit = lambda grad: jnp.pad(
        grad.reshape(count, padded, ff)[:, :rows_gu], ((0, 0), (0, max(rows_gu - padded, 0)), (0, 0))
    )
    grad_wgate, grad_wup = fit(outer(h2_all, grad_gate)), fit(outer(h2_all, grad_up))

    grad_x_one, grad_x_one_b, gain_two_grad, grad_attended = call(
        partial(residual_back_body, width),
        [((tokens, wide), F32), ((tokens, wide), BF), ((1, wide), F32), ((tokens, qd), BF)],
        grad_in_two, x_one, cot_rel, gain_two, *o_blocks,
        flops=2 * tokens * qd * width,
    )
    out_part = dot(hidden_act, down_weight)
    out_sum, _ = scatter_blocks(
        [after(out_part[j * tokens : (j + 1) * tokens], grad_attended) for j in range(count)]
    )
    output = to_natural(x_one, block, padded) + out_sum
    columns = lambda rows: [rows[:, j * padded : j * padded + block] for j in range(count)]
    dx_cols = exchange_blocks(columns(grad_x_one_b))
    h1_cols = jnp.concatenate(exchange_blocks(columns(after(first_input, h2_blocks[far]))), axis=0)
    attended_all = jnp.concatenate(gather_blocks(after(attended, h2_blocks[far])), axis=0)
    grad_q, dkv_part = call(
        partial(attend_back_body, count),
        [((tokens, qd), BF), ((total, 2 * kvd), BF)],
        query, attended, grad_attended, cosine, sine, *kv_all,
        scalars=(here,),
        flops=10 * tokens * qd * total,
    )
    dkv, dkv_sent = scatter_blocks([dkv_part[j * tokens : (j + 1) * tokens] for j in range(count)])
    (grad_kv,) = call(turn_keys_body, [((tokens, 2 * kvd), BF)], dkv, cosine, sine)

    rows_att = up_to(block, 8 * reps)
    pad_rows = lambda grad: jnp.pad(grad, ((0, rows_att - block), (0, 0)))
    dq_all = jnp.concatenate(gather_blocks(after(grad_q, dkv_sent)), axis=0)
    dkv_all = jnp.concatenate(gather_blocks(grad_kv), axis=0)
    grad_out = outer(jnp.concatenate([after(dx_cols[0], dkv_sent)] + dx_cols[1:], axis=0), attended_all)
    grad_qkv = jnp.concatenate([outer(h1_cols, dq_all), outer(h1_cols, dkv_all)], axis=1)
    gates = (dkv_sent, grad_kv, grad_qkv)
    down_share = rep_reduce(grad_down, 0, 0, gates)
    gate_share = rep_reduce(grad_wgate, 1, 1, gates)
    up_share = rep_reduce(grad_wup, 1, 0, gates)
    out_share = rep_reduce(pad_rows(grad_out), 0, 0, (grad_kv, grad_qkv))
    qkv_share = rep_reduce(pad_rows(grad_qkv), 0)
    grad_input, gain_one_grad, _ = call(
        partial(input_back_body, width, count),
        [((tokens, wide), F32), ((1, wide), F32), ((tokens, wide), F32)],
        after(grad_q, grad_qkv), grad_kv, x_rel, grad_x_one, gain_one, *q_blocks, *kv_blocks,
        flops=2 * tokens * width * (qd + 2 * kvd),
    )
    grad_input = to_natural(grad_input, block, padded)

    sum_down = rep_gather(down_share, 0).astype(F32)
    arrived = [
        exchange_blocks([share[j] for j in range(count)]) for share in (gate_share, up_share)
    ]
    sum_gate, sum_up = [
        rep_gather(jnp.concatenate(xor_blocks(blocks), axis=1), 0, first)[:block].astype(F32)
        for blocks, first in zip(arrived, (1, 0), strict=True)
    ]
    sum_out = rep_gather(out_share, 0)[:block].astype(F32).T
    sum_qkv = rep_gather(qkv_share, 0)[:block].astype(F32)

    both = jnp.concatenate([gain_one_grad, gain_two_grad], axis=0)
    kept = {j: both[:, j * padded : j * padded + block] for j in range(count)}
    bit = 1
    while bit < count:
        arrived = {j ^ bit: swap(kept[j], bit) for j in kept if j & bit}
        kept = {j: kept[j] + arrived[j] for j in arrived}
        bit *= 2
    gain_sum = kept[0]
    for bit in rep_bits():
        gain_sum = gain_sum + rep_swap(gain_sum, bit)
    return (
        output[None],
        grad_input[None],
        gain_sum[0],
        sum_qkv[:, :qd],
        sum_qkv[:, qd : qd + kvd],
        sum_qkv[:, qd + kvd :],
        sum_out,
        gain_sum[1],
        sum_gate,
        sum_up,
        sum_down,
    )


def solution(mesh):
    placed = (
        P("rep", "shard", None),
        P("rep", "shard", None),
        P("shard"),
        P("shard", None),
        P("shard", None),
        P("shard", None),
        P(None, "shard"),
        P("shard"),
        P("shard", None),
        P("shard", None),
        P("shard", None),
    )
    return jax.shard_map(
        local,
        mesh=mesh,
        in_specs=placed,
        out_specs=(
            P("rep", "shard", None),
            P("rep", "shard", None),
            P("shard"),
            P("shard", None),
            P("shard", None),
            P("shard", None),
            P(None, "shard"),
            P("shard"),
            P("shard", None),
            P("shard", None),
            P("shard", None),
        ),
        check_vma=False,
    )
```

```python
from functools import partial

import jax
import jax.numpy as jnp
from jax import lax
from jax.experimental import pallas as pl
from jax.experimental.pallas import tpu as pltpu
from jax.sharding import PartitionSpec as P

HEAD = 64
PER_KV = 3
EPSILON = 1e-05
SCALE = 0.125
NEGATIVE = -1e30
THETA = 10000.0
BF = jnp.bfloat16
F32 = jnp.float32


def dot(left, right):
    return jnp.dot(left, right, preferred_element_type=F32)


def outer(left, right):
    return lax.dot_general(left, right, (((0,), (0,)), ((), ())), preferred_element_type=F32)


def back(left, weight):
    return lax.dot_general(left, weight, (((1,), (1,)), ((), ())), preferred_element_type=F32)


def after(value, *earlier):
    return lax.optimization_barrier((value, *earlier))[0]


def up_to(size, unit):
    return -(-size // unit) * unit


def swap(value, mask):
    count = lax.axis_size("shard")
    return lax.ppermute(value, "shard", [(i, i ^ mask) for i in range(count)])


def gather_blocks(value, *gates):
    count = lax.axis_size("shard")
    blocks = {0: value}
    bit, level = count // 2, 0
    while bit:
        for j, block in list(blocks.items()):
            arrived = swap(block, bit)
            if level < len(gates) and gates[level] is not None:
                arrived = after(arrived, gates[level])
            blocks[j ^ bit] = arrived
        bit //= 2
        level += 1
    return [blocks[j] for j in range(count)]


def exchange_blocks(pieces):
    return [pieces[0]] + [swap(pieces[j], j) for j in range(1, len(pieces))]


def scatter_blocks(blocks, gate=None):
    count = len(blocks)
    kept = dict(enumerate(blocks))
    bit = 1
    while bit < count:
        sent = {j: kept[j].astype(BF) for j in kept if j & bit}
        arrived = {j ^ bit: swap(block, bit) for j, block in sent.items()}
        if gate is not None:
            arrived = {j: after(block, gate) for j, block in arrived.items()}
        kept = {j: kept[j].astype(F32) + arrived[j].astype(F32) for j in arrived}
        bit *= 2
    return kept[0], sent[count // 2]


def xor_blocks(blocks, place=None):
    shard, count = lax.axis_index("shard") if place is None else place, len(blocks)
    bit = 1
    while bit < count:
        odd = (shard & bit) != 0
        blocks = [jnp.where(odd, blocks[j ^ bit], blocks[j]) for j in range(count)]
        bit *= 2
    return blocks


def to_relative(rows, block, padded):
    count = rows.shape[1] // block
    blocks = xor_blocks([rows[:, j * block : (j + 1) * block] for j in range(count)])
    return jnp.concatenate([jnp.pad(b, ((0, 0), (0, padded - block))) for b in blocks], axis=1)


def to_natural(rows, block, padded):
    count = rows.shape[1] // padded
    blocks = xor_blocks([rows[:, j * padded : j * padded + block] for j in range(count)])
    return jnp.concatenate(blocks, axis=1)


def rep_swap(value, bit):
    count = lax.axis_size("rep")
    return lax.ppermute(value, "rep", [(i, i ^ bit) for i in range(count)])


def pair_quarters(pairs):
    rep = lax.axis_index("rep")
    second, fourth = (rep & 1) != 0, (rep & 2) != 0
    half = pairs[0][0].shape[0] // 2
    quarters = [jnp.where(second, two, one) for one, two in pairs[len(pairs) // 2 :]]
    return [jnp.where(fourth, q[half:], q[:half]) for q in quarters]


def complete_pairs(arrived, gate_with):
    rep = lax.axis_index("rep")
    second, fourth = (rep & 1) != 0, (rep & 2) != 0
    mine = jnp.stack(arrived)
    first_sent = mine
    theirs = after(rep_swap(mine, 2), gate_with(first_sent))
    mine = jnp.concatenate(
        [jnp.where(fourth, theirs, mine), jnp.where(fourth, mine, theirs)], axis=1
    )
    theirs = rep_swap(mine, 1)
    ones, twos = jnp.where(second, theirs, mine), jnp.where(second, mine, theirs)
    return mine, [(ones[k], twos[k]) for k in range(len(arrived))]


def rep_bits():
    count, bits, bit = lax.axis_size("rep"), [], 1
    while bit < count:
        bits.append(bit)
        bit *= 2
    return bits


def turned(bits, first):
    return bits[first : first + 1] + bits[:first] + bits[first + 1 :]


def rep_reduce(terms, axis, first=0, gates=()):
    rep, trail = lax.axis_index("rep"), []
    for step, bit in enumerate(turned(rep_bits(), first)):
        half = terms.shape[axis] // 2
        low = lax.slice_in_dim(terms, 0, half, axis=axis)
        high = lax.slice_in_dim(terms, half, 2 * half, axis=axis)
        odd = (rep & bit) != 0
        trail.append(jnp.where(odd, low, high).astype(BF))
        arrived = rep_swap(trail[-1], bit)
        if step < len(gates):
            arrived = after(arrived, gates[step])
        terms = (jnp.where(odd, high, low).astype(F32) + arrived.astype(F32)).astype(BF)
    return terms, trail


def rep_gather(share, first=0, gates=(), last=None):
    rep, trail = lax.axis_index("rep"), []
    for step, bit in enumerate(reversed(turned(rep_bits(), first))):
        trail.append(share)
        arrived = rep_swap(share, bit)
        if step < len(gates):
            arrived = after(arrived, gates[step])
        odd = (rep & bit) != 0
        if last is not None and step == len(rep_bits()) - 1:
            return last(odd, share, arrived), trail
        share = jnp.concatenate(
            [jnp.where(odd, arrived, share), jnp.where(odd, share, arrived)], axis=0
        )
    return share, trail


def finish_body(cuts, odd_ref, own_ref, arrived_ref, *outs):
    half = own_ref.shape[0]

    def write(low_ref, high_ref):
        for k, out_ref in enumerate(outs):
            turned_over = k == len(outs) - 1
            rows = out_ref.shape[1 if turned_over else 0]
            low = low_ref[: min(half, rows), cuts[k] : cuts[k + 1]].astype(F32)
            if turned_over:
                out_ref[:, : low.shape[0]] = low.T
            else:
                out_ref[: low.shape[0]] = low
            if rows > half:
                high = high_ref[: rows - half, cuts[k] : cuts[k + 1]].astype(F32)
                if turned_over:
                    out_ref[:, half:] = high.T
                else:
                    out_ref[half:] = high

    pl.when(odd_ref[0] == 1)(lambda: write(arrived_ref, own_ref))
    pl.when(odd_ref[0] == 0)(lambda: write(own_ref, arrived_ref))


def call(body, outs, *args, scalars=(), flops=0, scratch=(), limit=16 * 2**20):
    smem = [pl.BlockSpec(memory_space=pltpu.SMEM)] * len(scalars)
    vmem = [pl.BlockSpec(memory_space=pltpu.VMEM)] * len(args)
    shapes = [jax.ShapeDtypeStruct(shape, dtype) for shape, dtype in outs]
    moved = sum(a.size * a.dtype.itemsize for a in args)
    moved += sum(s.size * s.dtype.itemsize for s in shapes)
    return pl.pallas_call(
        body,
        out_shape=shapes,
        in_specs=smem + vmem,
        out_specs=[pl.BlockSpec(memory_space=pltpu.VMEM)] * len(outs),
        scratch_shapes=[pltpu.VMEM(shape, dtype) for shape, dtype in scratch],
        compiler_params=pltpu.CompilerParams(vmem_limit_bytes=limit),
        cost_estimate=pl.CostEstimate(flops=flops, bytes_accessed=moved, transcendentals=0),
    )(*scalars, *args)


def turn(head, cosine, sine):
    half = HEAD // 2
    swapped = jnp.concatenate([head[:, half:], head[:, :half]], axis=1)
    return head * cosine + swapped * sine


def normed(rows, width):
    inverse = lax.rsqrt(jnp.sum(rows * rows, axis=-1, keepdims=True) / width + EPSILON)
    return rows * inverse, inverse


def kv_body(width, x_ref, gain_ref, cos_ref, sin_ref, *refs):
    weights, (h_ref, kv_ref) = refs[:-2], refs[-2:]
    block = weights[0].shape[0]
    padded = x_ref.shape[1] // len(weights)
    rows, _ = normed(x_ref[...].astype(F32), width)
    h_ref[...] = (rows * gain_ref[...]).astype(BF)
    total = None
    for j, weight in enumerate(weights):
        term = dot(h_ref[:, j * padded : j * padded + block], weight[...])
        total = term if total is None else total + term
    kvd = total.shape[1] // 2
    for h in range(kvd // HEAD):
        head = total[:, h * HEAD : (h + 1) * HEAD]
        kv_ref[:, h * HEAD : (h + 1) * HEAD] = turn(head, cos_ref[...], sin_ref[...]).astype(BF)
    kv_ref[:, kvd:] = total[:, kvd:].astype(BF)


def allowed_keys(shard, tokens, total, rows):
    key = lax.broadcasted_iota(jnp.int32, (rows, total), 1)
    query = lax.broadcasted_iota(jnp.int32, (rows, total), 0)
    owner = (key // tokens) ^ shard
    return owner * tokens + key % tokens <= shard * tokens + query % tokens


def probabilities(query, key, allowed):
    scores = jnp.where(allowed, back(query * SCALE, key), NEGATIVE)
    weights = jnp.exp(scores - jnp.max(scores, axis=-1, keepdims=True))
    return weights * (1.0 / jnp.sum(weights, axis=-1, keepdims=True))


def arrange_body(*refs):
    blocks, out_ref = refs[:-1], refs[-1]
    count, (tokens, wide) = len(blocks), blocks[0].shape
    padded = wide // count
    for j, rows in enumerate(blocks):
        for i in range(count):
            out_ref[j * tokens : (j + 1) * tokens, i * padded : (i + 1) * padded] = rows[
                :, (i ^ j) * padded : ((i ^ j) + 1) * padded
            ]


def attend_body(count, shard_ref, h_ref, cos_ref, sin_ref, *refs):
    weights, kvs = refs[:count], refs[count : 2 * count]
    query_ref, attended_ref, group_ref, key_ref, value_ref = refs[2 * count :]
    tokens, block = h_ref.shape[0], weights[0].shape[0]
    padded = h_ref.shape[1] // count
    total = None
    for j, weight in enumerate(weights):
        term = dot(h_ref[:, j * padded : j * padded + block], weight[...])
        total = term if total is None else total + term
    for h in range(total.shape[1] // HEAD):
        head = total[:, h * HEAD : (h + 1) * HEAD]
        head = turn(head, cos_ref[...], sin_ref[...]).astype(BF)
        query_ref[:, h * HEAD : (h + 1) * HEAD] = head
        group_ref[h // PER_KV, (h % PER_KV) * tokens : (h % PER_KV + 1) * tokens] = head
    spread_kv(kvs, key_ref, value_ref)
    allowed = allowed_keys(shard_ref[0], tokens, tokens * count, tokens * PER_KV)

    @pl.loop(0, group_ref.shape[0])
    def _(g):
        prob = probabilities(group_ref[g], key_ref[g], allowed)
        group_ref[g] = dot(prob.astype(BF), value_ref[g]).astype(BF)

    gather_heads(group_ref, attended_ref)


def spread_kv(kvs, key_ref, value_ref):
    tokens, kvd = kvs[0].shape[0], kvs[0].shape[1] // 2
    for g in range(kvd // HEAD):
        low = g * HEAD
        for j, kv in enumerate(kvs):
            key_ref[g, j * tokens : (j + 1) * tokens] = kv[:, low : low + HEAD]
            value_ref[g, j * tokens : (j + 1) * tokens] = kv[:, kvd + low : kvd + low + HEAD]


def spread_heads(rows_ref, group_ref):
    tokens = rows_ref.shape[0]
    for h in range(rows_ref.shape[1] // HEAD):
        group_ref[h // PER_KV, (h % PER_KV) * tokens : (h % PER_KV + 1) * tokens] = rows_ref[
            :, h * HEAD : (h + 1) * HEAD
        ]


def gather_heads(group_ref, rows_ref):
    tokens = rows_ref.shape[0]
    for h in range(rows_ref.shape[1] // HEAD):
        rows_ref[:, h * HEAD : (h + 1) * HEAD] = group_ref[
            h // PER_KV, (h % PER_KV) * tokens : (h % PER_KV + 1) * tokens
        ]


def residual_body(width, attended_ref, x_ref, gain_ref, *refs):
    weights, (one_ref, h_ref) = refs[:-2], refs[-2:]
    block = weights[0].shape[0]
    padded = x_ref.shape[1] // len(weights)
    one_ref[...] = x_ref[...].astype(F32)
    for j, weight in enumerate(weights):
        one_ref[:, j * padded : j * padded + block] += back(attended_ref[...], weight[...])
    rows, _ = normed(one_ref[...], width)
    h_ref[...] = (rows * gain_ref[...]).astype(BF)


def norm_back(grad, rows, inverse, gain, width):
    scaled = grad * gain
    return inverse * (scaled - rows * (jnp.sum(scaled * rows, axis=-1, keepdims=True) / width))


def residual_back_body(width, grad_ref, one_ref, cot_ref, gain_ref, *refs):
    weights, (dx_ref, dxb_ref, gain_grad_ref, datt_ref) = refs[:-4], refs[-4:]
    block = weights[0].shape[0]
    padded = one_ref.shape[1] // len(weights)
    rows, inverse = normed(one_ref[...], width)
    grad = grad_ref[...]
    gain_grad_ref[...] = jnp.sum(grad * rows, axis=0, keepdims=True)
    dx_ref[...] = cot_ref[...].astype(F32) + norm_back(grad, rows, inverse, gain_ref[...], width)
    dxb_ref[...] = dx_ref[...].astype(BF)
    total = None
    for j, weight in enumerate(weights):
        term = dot(dxb_ref[:, j * padded : j * padded + block], weight[...])
        total = term if total is None else total + term
    datt_ref[...] = total.astype(BF)


def attend_back_body(count, shard_ref, query_ref, att_ref, datt_ref, cos_ref, sin_ref, *refs):
    kvs = refs[:count]
    dq_ref, dkv_ref, qs_ref, atts_ref, datts_ref, key_ref, value_ref = refs[count:]
    tokens = query_ref.shape[0]
    kvd = kvs[0].shape[1] // 2
    spread_kv(kvs, key_ref, value_ref)
    spread_heads(query_ref, qs_ref)
    spread_heads(att_ref, atts_ref)
    spread_heads(datt_ref, datts_ref)
    allowed = allowed_keys(shard_ref[0], tokens, tokens * count, tokens * PER_KV)

    @pl.loop(0, qs_ref.shape[0])
    def _(g):
        query, key, value, datt = qs_ref[g], key_ref[g], value_ref[g], datts_ref[g]
        prob = probabilities(query, key, allowed)
        delta = jnp.sum(datt.astype(F32) * atts_ref[g].astype(F32), axis=-1, keepdims=True)
        dscore = (prob * (back(datt, value) - delta) * SCALE).astype(BF)
        value_ref[g] = outer(prob.astype(BF), datt).astype(BF)
        key_ref[g] = outer(dscore, query).astype(BF)
        rows = dot(dscore, key)
        for k in range(PER_KV):
            head = rows[k * tokens : (k + 1) * tokens]
            atts_ref[g, k * tokens : (k + 1) * tokens] = turn(
                head, cos_ref[...], -sin_ref[...]
            ).astype(BF)

    gather_heads(atts_ref, dq_ref)
    for g in range(kvd // HEAD):
        low = g * HEAD
        dkv_ref[:, low : low + HEAD] = key_ref[g]
        dkv_ref[:, kvd + low : kvd + low + HEAD] = value_ref[g]


def turn_keys_body(dkv_ref, cos_ref, sin_ref, out_ref):
    kvd = dkv_ref.shape[1] // 2
    for h in range(kvd // HEAD):
        head = dkv_ref[:, h * HEAD : (h + 1) * HEAD]
        out_ref[:, h * HEAD : (h + 1) * HEAD] = turn(head, cos_ref[...], -sin_ref[...]).astype(BF)
    out_ref[:, kvd:] = dkv_ref[:, kvd:].astype(BF)


def input_back_body(width, count, dq_ref, dkv_ref, x_ref, dx_ref, gain_ref, *refs):
    wqs, wkvs = refs[:count], refs[count : 2 * count]
    out_ref, gain_grad_ref, grad_ref = refs[2 * count :]
    block = wqs[0].shape[0]
    padded = x_ref.shape[1] // count
    grad_ref[...] = jnp.zeros_like(grad_ref)
    for j in range(count):
        grad_ref[:, j * padded : j * padded + block] = back(dq_ref[...], wqs[j][...]) + back(
            dkv_ref[...], wkvs[j][...]
        )
    rows, inverse = normed(x_ref[...].astype(F32), width)
    grad = grad_ref[...]
    gain_grad_ref[...] = jnp.sum(grad * rows, axis=0, keepdims=True)
    out_ref[...] = dx_ref[...] + norm_back(grad, rows, inverse, gain_ref[...], width)


def local(
    hidden_in,
    out_grad,
    norm1_gain,
    q_weight,
    k_weight,
    v_weight,
    o_weight,
    norm2_gain,
    gate_weight,
    up_weight,
    down_weight,
):
    shard, count = lax.axis_index("shard"), lax.axis_size("shard")
    reps = lax.axis_size("rep")
    tokens, width = hidden_in.shape[1:]
    block = q_weight.shape[0]
    padded = up_to(block, 128)
    wide = count * padded
    qd, kvd = q_weight.shape[1], k_weight.shape[1]
    ff = down_weight.shape[0]
    total = tokens * count
    far = count // 2
    here = shard.astype(jnp.int32)[None]
    grouped = ((kvd // HEAD, PER_KV * tokens, HEAD), BF)
    keyed = ((kvd // HEAD, total, HEAD), BF)
    room = 12 * 2**20 + 32 * PER_KV * tokens * total

    kv_held = jnp.concatenate([k_weight, v_weight], axis=1)
    kv_blocks = gather_blocks(kv_held)
    gains = gather_blocks(jnp.pad(jnp.stack([norm1_gain, norm2_gain]), ((0, 0), (0, padded - block))))
    gains = jnp.concatenate(gains, axis=1).astype(F32)
    gain_one, gain_two = gains[:1], gains[1:]

    positions = (shard * tokens + jnp.arange(tokens, dtype=jnp.int32)).astype(F32)
    freqs = THETA ** (-(jnp.arange(HEAD // 2, dtype=F32) * 2.0 / HEAD))
    angles = positions[:, None] * freqs[None, :]
    cosine, sine = jnp.cos(angles), jnp.sin(angles)
    cosine = jnp.concatenate([cosine, cosine], axis=1)
    sine = jnp.concatenate([-sine, sine], axis=1)

    split = lambda rows: xor_blocks([rows[:, j * ff : (j + 1) * ff] for j in range(count)])
    pairs = list(zip(split(gate_weight), split(up_weight), strict=True))
    assisted = len(rep_bits()) >= 2
    crossing = pair_quarters(pairs) if assisted else []
    x_rel = to_relative(hidden_in[0], block, padded)
    cot_rel = to_relative(out_grad[0], block, padded)
    o_turned = o_weight.T
    ready = (q_weight, *crossing, kv_blocks[far], x_rel, cot_rel, o_turned)
    q_held, *crossing = lax.optimization_barrier(ready)[: 1 + len(crossing)]
    first_input, kv_own = call(
        partial(kv_body, width),
        [((tokens, wide), BF), ((tokens, 2 * kvd), BF)],
        x_rel, gain_one, cosine, sine, *kv_blocks,
        flops=4 * tokens * width * kvd,
    )
    kv_all = gather_blocks(kv_own)
    q_blocks = gather_blocks(q_held, kv_own)
    crossed = [after(swap(q, far + k), kv_own) for k, q in enumerate(crossing)]
    o_held, *near = lax.optimization_barrier(
        (o_turned, *[p for pair in pairs[1 : far if assisted else count] for p in pair], q_blocks[far], kv_all[far])
    )[:-2]
    o_blocks = gather_blocks(o_held)
    attention = []

    def attend(*sent):
        attention.extend(
            call(
                partial(attend_body, count),
                [((tokens, qd), BF), ((tokens, qd), BF)],
                after(first_input, *sent), cosine, sine, *q_blocks, *kv_all,
                scalars=(here,),
                flops=2 * tokens * qd * (width + 2 * total),
                scratch=[grouped, keyed, keyed], limit=room,
            )
        )
        return attention[1]

    if assisted:
        completing, far_pairs = complete_pairs(crossed, attend)
    else:
        completing, far_pairs = attend(), []
    query, attended = attention
    near = [swap(p, 1 + k // 2) for k, p in enumerate(near)]
    all_pairs = [pairs[0], *zip(near[::2], near[1::2], strict=True), *far_pairs]
    gate_blocks, up_blocks = zip(*all_pairs, strict=True)
    x_one, input_two = call(
        partial(residual_body, width),
        [((tokens, wide), F32), ((tokens, wide), BF)],
        after(attended, completing), x_rel, gain_two, *o_blocks,
        flops=2 * tokens * qd * width,
    )

    joined = lambda blocks: jnp.concatenate(
        [jnp.pad(b, ((0, padded - block), (0, 0))) for b in blocks], axis=0
    )
    w_gate, w_up = joined(gate_blocks), joined(up_blocks)
    og_all = jnp.concatenate(gather_blocks(after(out_grad[0], o_blocks[far])), axis=0)

    reorder = lambda rows, j: jnp.concatenate(
        [rows[:, (i ^ j) * padded : ((i ^ j) + 1) * padded] for i in range(count)], axis=1
    )
    h2_blocks = gather_blocks(input_two)
    (h2_all,) = call(arrange_body, [((total, wide), BF)], *h2_blocks)
    grad_hidden = back(og_all, down_weight)
    gate, upward = dot(h2_all, w_gate), dot(h2_all, w_up)
    sigma = jax.nn.sigmoid(gate)
    silu_gate = gate * sigma
    hidden_act = (silu_gate * upward).astype(BF)
    grad_gate = (grad_hidden * upward * sigma * (1.0 + gate * (1.0 - sigma))).astype(BF)
    grad_up = (grad_hidden * silu_gate).astype(BF)
    dh2_part = (back(grad_gate, w_gate) + back(grad_up, w_up)).astype(BF)
    grad_in_two, dh2_sent = scatter_blocks(
        [reorder(dh2_part[j * tokens : (j + 1) * tokens], j) for j in range(count)]
    )
    grad_down = outer(hidden_act, og_all).astype(BF)
    rows_gu = up_to(block, 8 * reps)
    fit = lambda grad: jnp.pad(
        grad.reshape(count, padded, ff)[:, :rows_gu], ((0, 0), (0, max(rows_gu - padded, 0)), (0, 0))
    )
    grad_wgate, grad_wup = fit(outer(h2_all, grad_gate).astype(BF)), fit(outer(h2_all, grad_up).astype(BF))

    grad_x_one, grad_x_one_b, gain_two_grad, grad_attended = call(
        partial(residual_back_body, width),
        [((tokens, wide), F32), ((tokens, wide), BF), ((1, wide), F32), ((tokens, qd), BF)],
        grad_in_two, x_one, cot_rel, gain_two, *o_blocks,
        flops=2 * tokens * qd * width,
    )
    out_part = dot(hidden_act, down_weight)
    columns = lambda rows: [rows[:, j * padded : j * padded + block] for j in range(count)]
    dx_cols = exchange_blocks(columns(grad_x_one_b))
    h1_blocks = exchange_blocks(columns(after(first_input, hidden_act)))
    attended_blocks = gather_blocks(after(attended, hidden_act), grad_down)
    grad_q, dkv_part = call(
        partial(attend_back_body, count),
        [((tokens, qd), BF), ((total, 2 * kvd), BF)],
        query, attended, grad_attended, cosine, sine, *kv_all,
        scalars=(here,),
        flops=10 * tokens * qd * total,
        scratch=[grouped] * 3 + [keyed] * 2, limit=room,
    )
    dkv, dkv_sent = scatter_blocks([dkv_part[j * tokens : (j + 1) * tokens] for j in range(count)])
    out_sum, _ = scatter_blocks(
        [after(out_part[j * tokens : (j + 1) * tokens], grad_attended) for j in range(count)], dkv_sent
    )
    output = to_natural(x_one, block, padded) + out_sum
    (grad_kv,) = call(turn_keys_body, [((tokens, 2 * kvd), BF)], dkv, cosine, sine)

    rows_att = up_to(block, 8 * reps)
    pad_rows = lambda grad: jnp.pad(grad, ((0, rows_att - block), (0, 0)))
    dq_blocks = gather_blocks(after(grad_q, dkv_sent), grad_kv)
    dkv_blocks = gather_blocks(grad_kv)
    attended_all, h1_cols, dx_cols = [
        jnp.concatenate([after(blocks[0], grad_kv), *blocks[1:]], axis=0)
        for blocks in (attended_blocks, h1_blocks, dx_cols)
    ]
    dqkv_all = [jnp.concatenate(blocks, axis=0) for blocks in (dq_blocks, dkv_blocks)]
    grad_att = pad_rows(
        jnp.concatenate(
            [outer(h1_cols, rows).astype(BF) for rows in dqkv_all]
            + [outer(dx_cols, attended_all).astype(BF)],
            axis=1,
        )
    )
    att_share, trail = rep_reduce(grad_att, 0)
    gates = (dkv_sent, grad_kv, trail[min(1, len(trail) - 1)])
    down_share, _ = rep_reduce(after(grad_down, dh2_sent), 0, 1, gates)
    gate_share, _ = rep_reduce(after(grad_wgate, dh2_sent), 1, 1, gates)
    up_share, _ = rep_reduce(after(grad_wup, dh2_sent), 1, 0, gates)

    cuts = (0, qd, qd + kvd, qd + 2 * kvd, 2 * qd + 2 * kvd)
    finish = lambda odd, own, arrived: call(
        partial(finish_body, cuts),
        [((block, qd), F32), ((block, kvd), F32), ((block, kvd), F32), ((qd, block), F32)],
        own,
        arrived,
        scalars=(odd.astype(jnp.int32)[None],),
    )
    sum_att, trail_back = rep_gather(att_share, 0, (), finish)
    gates = (trail[-1], *trail_back)
    sum_down = rep_gather(down_share, 1, gates)[0].astype(F32)
    shares = jnp.concatenate([gate_share, up_share], axis=2)
    blocks = exchange_blocks([shares[j] for j in range(count)])
    (sum_gate, _), (sum_up, _) = [
        rep_gather(
            jnp.concatenate(xor_blocks([b[:, k * ff : (k + 1) * ff] for b in blocks]), axis=1),
            1 - k, gates,
        )
        for k in range(2)
    ]
    sum_gate, sum_up = sum_gate[:block].astype(F32), sum_up[:block].astype(F32)
    grad_input, gain_one_grad, _ = call(
        partial(input_back_body, width, count),
        [((tokens, wide), F32), ((1, wide), F32), ((tokens, wide), F32)],
        after(grad_q, trail[-1]), grad_kv, x_rel, grad_x_one, gain_one, *q_blocks, *kv_blocks,
        flops=2 * tokens * width * (qd + 2 * kvd),
    )
    grad_input = to_natural(grad_input, block, padded)

    both = jnp.concatenate([gain_one_grad, gain_two_grad], axis=0)
    arrived = exchange_blocks(columns(both))
    gain_sum = sum([after(b, trail_back[0]) for b in arrived[1:]], arrived[0])
    for step, bit in enumerate(rep_bits()):
        arrived = rep_swap(gain_sum, bit)
        if step + 1 < len(trail_back):
            arrived = after(arrived, trail_back[step + 1])
        gain_sum = gain_sum + arrived
    return (
        output[None],
        grad_input[None],
        gain_sum[0],
        *sum_att,
        gain_sum[1],
        sum_gate,
        sum_up,
        sum_down,
    )


def solution(mesh):
    placed = (
        P("rep", "shard", None),
        P("rep", "shard", None),
        P("shard"),
        P("shard", None),
        P("shard", None),
        P("shard", None),
        P(None, "shard"),
        P("shard"),
        P("shard", None),
        P("shard", None),
        P("shard", None),
    )
    return jax.shard_map(
        local,
        mesh=mesh,
        in_specs=placed,
        out_specs=(
            P("rep", "shard", None),
            P("rep", "shard", None),
            P("shard"),
            P("shard", None),
            P("shard", None),
            P("shard", None),
            P(None, "shard"),
            P("shard"),
            P("shard", None),
            P("shard", None),
            P("shard", None),
        ),
        check_vma=False,
    )
```

```python
from functools import partial

import jax
import jax.numpy as jnp
from jax import lax
from jax.experimental import pallas as pl
from jax.experimental.pallas import tpu as pltpu
from jax.sharding import PartitionSpec as P

HEAD = 64
PER_KV = 3
EPSILON = 1e-05
SCALE = 0.125
NEGATIVE = -1e30
THETA = 10000.0
BF = jnp.bfloat16
F32 = jnp.float32


def dot(left, right):
    return jnp.dot(left, right, preferred_element_type=F32)


def outer(left, right):
    return lax.dot_general(left, right, (((0,), (0,)), ((), ())), preferred_element_type=F32)


def back(left, weight):
    return lax.dot_general(left, weight, (((1,), (1,)), ((), ())), preferred_element_type=F32)


def after(value, *earlier):
    return lax.optimization_barrier((value, *earlier))[0]


def up_to(size, unit):
    return -(-size // unit) * unit


def swap(value, mask):
    count = lax.axis_size("shard")
    return lax.ppermute(value, "shard", [(i, i ^ mask) for i in range(count)])


def gather_blocks(value, *gates):
    count = lax.axis_size("shard")
    blocks = {0: value}
    bit, level = count // 2, 0
    while bit:
        for j, block in list(blocks.items()):
            arrived = swap(block, bit)
            if level < len(gates) and gates[level] is not None:
                arrived = after(arrived, gates[level])
            blocks[j ^ bit] = arrived
        bit //= 2
        level += 1
    return [blocks[j] for j in range(count)]


def exchange_blocks(pieces):
    return [pieces[0]] + [swap(pieces[j], j) for j in range(1, len(pieces))]


def scatter_blocks(blocks, gate=None):
    count = len(blocks)
    kept = dict(enumerate(blocks))
    bit = 1
    while bit < count:
        sent = {j: kept[j].astype(BF) for j in kept if j & bit}
        arrived = {j ^ bit: swap(block, bit) for j, block in sent.items()}
        if gate is not None:
            arrived = {j: after(block, gate) for j, block in arrived.items()}
        kept = {j: kept[j].astype(F32) + arrived[j].astype(F32) for j in arrived}
        bit *= 2
    return kept[0], sent[count // 2]


def xor_blocks(blocks, place=None):
    shard, count = lax.axis_index("shard") if place is None else place, len(blocks)
    bit = 1
    while bit < count:
        odd = (shard & bit) != 0
        blocks = [jnp.where(odd, blocks[j ^ bit], blocks[j]) for j in range(count)]
        bit *= 2
    return blocks


def to_relative(rows, block, padded):
    count = rows.shape[1] // block
    blocks = xor_blocks([rows[:, j * block : (j + 1) * block] for j in range(count)])
    return jnp.concatenate([jnp.pad(b, ((0, 0), (0, padded - block))) for b in blocks], axis=1)


def to_natural(rows, block, padded):
    count = rows.shape[1] // padded
    blocks = xor_blocks([rows[:, j * padded : j * padded + block] for j in range(count)])
    return jnp.concatenate(blocks, axis=1)


def rep_swap(value, bit):
    count = lax.axis_size("rep")
    return lax.ppermute(value, "rep", [(i, i ^ bit) for i in range(count)])


def pair_quarters(pairs):
    rep = lax.axis_index("rep")
    second, fourth = (rep & 1) != 0, (rep & 2) != 0
    half = pairs[0][0].shape[0] // 2
    quarters = [jnp.where(second, two, one) for one, two in pairs[len(pairs) // 2 :]]
    return [jnp.where(fourth, q[half:], q[:half]) for q in quarters]


def complete_pairs(arrived, gate_with):
    rep = lax.axis_index("rep")
    second, fourth = (rep & 1) != 0, (rep & 2) != 0
    mine = jnp.stack(arrived)
    first_sent = mine
    theirs = after(rep_swap(mine, 2), gate_with(first_sent))
    mine = jnp.concatenate(
        [jnp.where(fourth, theirs, mine), jnp.where(fourth, mine, theirs)], axis=1
    )
    theirs = rep_swap(mine, 1)
    ones, twos = jnp.where(second, theirs, mine), jnp.where(second, mine, theirs)
    return mine, [(ones[k], twos[k]) for k in range(len(arrived))]


def rep_bits():
    count, bits, bit = lax.axis_size("rep"), [], 1
    while bit < count:
        bits.append(bit)
        bit *= 2
    return bits


def turned(bits, first):
    return bits[first : first + 1] + bits[:first] + bits[first + 1 :]


def rep_reduce(terms, axis, first=0, gates=()):
    rep, trail = lax.axis_index("rep"), []
    for step, bit in enumerate(turned(rep_bits(), first)):
        half = terms.shape[axis] // 2
        low = lax.slice_in_dim(terms, 0, half, axis=axis)
        high = lax.slice_in_dim(terms, half, 2 * half, axis=axis)
        odd = (rep & bit) != 0
        trail.append(jnp.where(odd, low, high).astype(BF))
        arrived = rep_swap(trail[-1], bit)
        if step < len(gates):
            arrived = after(arrived, gates[step])
        terms = (jnp.where(odd, high, low).astype(F32) + arrived.astype(F32)).astype(BF)
    return terms, trail


def rep_gather(share, first=0, gates=(), last=None):
    rep, trail = lax.axis_index("rep"), []
    for step, bit in enumerate(reversed(turned(rep_bits(), first))):
        trail.append(share)
        arrived = rep_swap(share, bit)
        if step < len(gates):
            arrived = after(arrived, gates[step])
        odd = (rep & bit) != 0
        if last is not None and step == len(rep_bits()) - 1:
            return last(odd, share, arrived), trail
        share = jnp.concatenate(
            [jnp.where(odd, arrived, share), jnp.where(odd, share, arrived)], axis=0
        )
    return share, trail


def finish_body(cuts, flip, odd_ref, own_ref, arrived_ref, *outs):
    half = own_ref.shape[0]

    def write(low_ref, high_ref):
        for k, out_ref in enumerate(outs):
            turned_over = flip and k == len(outs) - 1
            rows = out_ref.shape[1 if turned_over else 0]
            low = low_ref[: min(half, rows), cuts[k] : cuts[k + 1]].astype(F32)
            if turned_over:
                out_ref[:, : low.shape[0]] = low.T
            else:
                out_ref[: low.shape[0]] = low
            if rows > half:
                high = high_ref[: rows - half, cuts[k] : cuts[k + 1]].astype(F32)
                if turned_over:
                    out_ref[:, half:] = high.T
                else:
                    out_ref[half:] = high

    pl.when(odd_ref[0] == 1)(lambda: write(arrived_ref, own_ref))
    pl.when(odd_ref[0] == 0)(lambda: write(own_ref, arrived_ref))


def call(body, outs, *args, scalars=(), flops=0, scratch=(), limit=16 * 2**20):
    smem = [pl.BlockSpec(memory_space=pltpu.SMEM)] * len(scalars)
    vmem = [pl.BlockSpec(memory_space=pltpu.VMEM)] * len(args)
    shapes = [jax.ShapeDtypeStruct(shape, dtype) for shape, dtype in outs]
    moved = sum(a.size * a.dtype.itemsize for a in args)
    moved += sum(s.size * s.dtype.itemsize for s in shapes)
    return pl.pallas_call(
        body,
        out_shape=shapes,
        in_specs=smem + vmem,
        out_specs=[pl.BlockSpec(memory_space=pltpu.VMEM)] * len(outs),
        scratch_shapes=[pltpu.VMEM(shape, dtype) for shape, dtype in scratch],
        compiler_params=pltpu.CompilerParams(vmem_limit_bytes=limit),
        cost_estimate=pl.CostEstimate(flops=flops, bytes_accessed=moved, transcendentals=0),
    )(*scalars, *args)


def turn(head, cosine, sine):
    half = HEAD // 2
    swapped = jnp.concatenate([head[:, half:], head[:, :half]], axis=1)
    return head * cosine + swapped * sine


def normed(rows, width):
    inverse = lax.rsqrt(jnp.sum(rows * rows, axis=-1, keepdims=True) / width + EPSILON)
    return rows * inverse, inverse


def kv_body(width, x_ref, gain_ref, cos_ref, sin_ref, *refs):
    weights, (h_ref, kv_ref) = refs[:-2], refs[-2:]
    block = weights[0].shape[0]
    padded = x_ref.shape[1] // len(weights)
    rows, _ = normed(x_ref[...].astype(F32), width)
    h_ref[...] = (rows * gain_ref[...]).astype(BF)
    total = None
    for j, weight in enumerate(weights):
        term = dot(h_ref[:, j * padded : j * padded + block], weight[...])
        total = term if total is None else total + term
    kvd = total.shape[1] // 2
    for h in range(kvd // HEAD):
        head = total[:, h * HEAD : (h + 1) * HEAD]
        kv_ref[:, h * HEAD : (h + 1) * HEAD] = turn(head, cos_ref[...], sin_ref[...]).astype(BF)
    kv_ref[:, kvd:] = total[:, kvd:].astype(BF)


def allowed_keys(shard, tokens, total, rows):
    key = lax.broadcasted_iota(jnp.int32, (rows, total), 1)
    query = lax.broadcasted_iota(jnp.int32, (rows, total), 0)
    owner = (key // tokens) ^ shard
    return owner * tokens + key % tokens <= shard * tokens + query % tokens


def probabilities(query, key, allowed):
    scores = jnp.where(allowed, back(query * SCALE, key), NEGATIVE)
    weights = jnp.exp(scores - jnp.max(scores, axis=-1, keepdims=True))
    return weights * (1.0 / jnp.sum(weights, axis=-1, keepdims=True))


def arrange_body(*refs):
    blocks, out_ref = refs[:-1], refs[-1]
    count, (tokens, wide) = len(blocks), blocks[0].shape
    padded = wide // count
    for j, rows in enumerate(blocks):
        for i in range(count):
            out_ref[j * tokens : (j + 1) * tokens, i * padded : (i + 1) * padded] = rows[
                :, (i ^ j) * padded : ((i ^ j) + 1) * padded
            ]


def attend_body(count, shard_ref, h_ref, cos_ref, sin_ref, *refs):
    weights, kvs = refs[:count], refs[count : 2 * count]
    query_ref, attended_ref, group_ref, key_ref, value_ref = refs[2 * count :]
    tokens, block = h_ref.shape[0], weights[0].shape[0]
    padded = h_ref.shape[1] // count
    total = None
    for j, weight in enumerate(weights):
        term = dot(h_ref[:, j * padded : j * padded + block], weight[...])
        total = term if total is None else total + term
    for h in range(total.shape[1] // HEAD):
        head = total[:, h * HEAD : (h + 1) * HEAD]
        head = turn(head, cos_ref[...], sin_ref[...]).astype(BF)
        query_ref[:, h * HEAD : (h + 1) * HEAD] = head
        group_ref[h // PER_KV, (h % PER_KV) * tokens : (h % PER_KV + 1) * tokens] = head
    spread_kv(kvs, key_ref, value_ref)
    allowed = allowed_keys(shard_ref[0], tokens, tokens * count, tokens * PER_KV)

    @pl.loop(0, group_ref.shape[0])
    def _(g):
        prob = probabilities(group_ref[g], key_ref[g], allowed)
        group_ref[g] = dot(prob.astype(BF), value_ref[g]).astype(BF)

    gather_heads(group_ref, attended_ref)


def spread_kv(kvs, key_ref, value_ref):
    tokens, kvd = kvs[0].shape[0], kvs[0].shape[1] // 2
    for g in range(kvd // HEAD):
        low = g * HEAD
        for j, kv in enumerate(kvs):
            key_ref[g, j * tokens : (j + 1) * tokens] = kv[:, low : low + HEAD]
            value_ref[g, j * tokens : (j + 1) * tokens] = kv[:, kvd + low : kvd + low + HEAD]


def spread_heads(rows_ref, group_ref):
    tokens = rows_ref.shape[0]
    for h in range(rows_ref.shape[1] // HEAD):
        group_ref[h // PER_KV, (h % PER_KV) * tokens : (h % PER_KV + 1) * tokens] = rows_ref[
            :, h * HEAD : (h + 1) * HEAD
        ]


def gather_heads(group_ref, rows_ref):
    tokens = rows_ref.shape[0]
    for h in range(rows_ref.shape[1] // HEAD):
        rows_ref[:, h * HEAD : (h + 1) * HEAD] = group_ref[
            h // PER_KV, (h % PER_KV) * tokens : (h % PER_KV + 1) * tokens
        ]


def residual_body(width, attended_ref, x_ref, gain_ref, *refs):
    weights, (one_ref, h_ref) = refs[:-2], refs[-2:]
    block = weights[0].shape[0]
    padded = x_ref.shape[1] // len(weights)
    one_ref[...] = x_ref[...].astype(F32)
    for j, weight in enumerate(weights):
        one_ref[:, j * padded : j * padded + block] += back(attended_ref[...], weight[...])
    rows, _ = normed(one_ref[...], width)
    h_ref[...] = (rows * gain_ref[...]).astype(BF)


def norm_back(grad, rows, inverse, gain, width):
    scaled = grad * gain
    return inverse * (scaled - rows * (jnp.sum(scaled * rows, axis=-1, keepdims=True) / width))


def residual_back_body(width, grad_ref, one_ref, cot_ref, gain_ref, *refs):
    weights, (dx_ref, dxb_ref, gain_grad_ref, datt_ref) = refs[:-4], refs[-4:]
    block = weights[0].shape[0]
    padded = one_ref.shape[1] // len(weights)
    rows, inverse = normed(one_ref[...], width)
    grad = grad_ref[...]
    gain_grad_ref[...] = jnp.sum(grad * rows, axis=0, keepdims=True)
    dx_ref[...] = cot_ref[...].astype(F32) + norm_back(grad, rows, inverse, gain_ref[...], width)
    dxb_ref[...] = dx_ref[...].astype(BF)
    total = None
    for j, weight in enumerate(weights):
        term = dot(dxb_ref[:, j * padded : j * padded + block], weight[...])
        total = term if total is None else total + term
    datt_ref[...] = total.astype(BF)


def attend_back_body(count, shard_ref, query_ref, att_ref, datt_ref, cos_ref, sin_ref, *refs):
    kvs = refs[:count]
    dq_ref, dkv_ref, qs_ref, atts_ref, datts_ref, key_ref, value_ref = refs[count:]
    tokens = query_ref.shape[0]
    kvd = kvs[0].shape[1] // 2
    spread_kv(kvs, key_ref, value_ref)
    spread_heads(query_ref, qs_ref)
    spread_heads(att_ref, atts_ref)
    spread_heads(datt_ref, datts_ref)
    allowed = allowed_keys(shard_ref[0], tokens, tokens * count, tokens * PER_KV)

    @pl.loop(0, qs_ref.shape[0])
    def _(g):
        query, key, value, datt = qs_ref[g], key_ref[g], value_ref[g], datts_ref[g]
        prob = probabilities(query, key, allowed)
        delta = jnp.sum(datt.astype(F32) * atts_ref[g].astype(F32), axis=-1, keepdims=True)
        dscore = (prob * (back(datt, value) - delta) * SCALE).astype(BF)
        value_ref[g] = outer(prob.astype(BF), datt).astype(BF)
        key_ref[g] = outer(dscore, query).astype(BF)
        rows = dot(dscore, key)
        for k in range(PER_KV):
            head = rows[k * tokens : (k + 1) * tokens]
            atts_ref[g, k * tokens : (k + 1) * tokens] = turn(
                head, cos_ref[...], -sin_ref[...]
            ).astype(BF)

    gather_heads(atts_ref, dq_ref)
    for g in range(kvd // HEAD):
        low = g * HEAD
        dkv_ref[:, low : low + HEAD] = key_ref[g]
        dkv_ref[:, kvd + low : kvd + low + HEAD] = value_ref[g]


def turn_keys_body(dkv_ref, cos_ref, sin_ref, out_ref):
    kvd = dkv_ref.shape[1] // 2
    for h in range(kvd // HEAD):
        head = dkv_ref[:, h * HEAD : (h + 1) * HEAD]
        out_ref[:, h * HEAD : (h + 1) * HEAD] = turn(head, cos_ref[...], -sin_ref[...]).astype(BF)
    out_ref[:, kvd:] = dkv_ref[:, kvd:].astype(BF)


def input_back_body(width, count, dq_ref, dkv_ref, x_ref, dx_ref, gain_ref, *refs):
    wqs, wkvs = refs[:count], refs[count : 2 * count]
    out_ref, gain_grad_ref, grad_ref = refs[2 * count :]
    block = wqs[0].shape[0]
    padded = x_ref.shape[1] // count
    grad_ref[...] = jnp.zeros_like(grad_ref)
    for j in range(count):
        grad_ref[:, j * padded : j * padded + block] = back(dq_ref[...], wqs[j][...]) + back(
            dkv_ref[...], wkvs[j][...]
        )
    rows, inverse = normed(x_ref[...].astype(F32), width)
    grad = grad_ref[...]
    gain_grad_ref[...] = jnp.sum(grad * rows, axis=0, keepdims=True)
    out_ref[...] = dx_ref[...] + norm_back(grad, rows, inverse, gain_ref[...], width)


def local(
    hidden_in,
    out_grad,
    norm1_gain,
    q_weight,
    k_weight,
    v_weight,
    o_weight,
    norm2_gain,
    gate_weight,
    up_weight,
    down_weight,
):
    shard, count = lax.axis_index("shard"), lax.axis_size("shard")
    reps = lax.axis_size("rep")
    tokens, width = hidden_in.shape[1:]
    block = q_weight.shape[0]
    padded = up_to(block, 128)
    wide = count * padded
    qd, kvd = q_weight.shape[1], k_weight.shape[1]
    ff = down_weight.shape[0]
    total = tokens * count
    far = count // 2
    here = shard.astype(jnp.int32)[None]
    grouped = ((kvd // HEAD, PER_KV * tokens, HEAD), BF)
    keyed = ((kvd // HEAD, total, HEAD), BF)
    room = 12 * 2**20 + 32 * PER_KV * tokens * total

    kv_held = jnp.concatenate([k_weight, v_weight], axis=1)
    kv_blocks = gather_blocks(kv_held)
    gains = gather_blocks(jnp.pad(jnp.stack([norm1_gain, norm2_gain]), ((0, 0), (0, padded - block))))
    gains = jnp.concatenate(gains, axis=1).astype(F32)
    gain_one, gain_two = gains[:1], gains[1:]

    positions = (shard * tokens + jnp.arange(tokens, dtype=jnp.int32)).astype(F32)
    freqs = THETA ** (-(jnp.arange(HEAD // 2, dtype=F32) * 2.0 / HEAD))
    angles = positions[:, None] * freqs[None, :]
    cosine, sine = jnp.cos(angles), jnp.sin(angles)
    cosine = jnp.concatenate([cosine, cosine], axis=1)
    sine = jnp.concatenate([-sine, sine], axis=1)

    split = lambda rows: xor_blocks([rows[:, j * ff : (j + 1) * ff] for j in range(count)])
    pairs = list(zip(split(gate_weight), split(up_weight), strict=True))
    assisted = len(rep_bits()) >= 2
    crossing = pair_quarters(pairs) if assisted else []
    x_rel = to_relative(hidden_in[0], block, padded)
    cot_rel = to_relative(out_grad[0], block, padded)
    o_turned = o_weight.T
    ready = (q_weight, *crossing, kv_blocks[far], x_rel, cot_rel, o_turned)
    q_held, *crossing = lax.optimization_barrier(ready)[: 1 + len(crossing)]
    first_input, kv_own = call(
        partial(kv_body, width),
        [((tokens, wide), BF), ((tokens, 2 * kvd), BF)],
        x_rel, gain_one, cosine, sine, *kv_blocks,
        flops=4 * tokens * width * kvd,
    )
    kv_all = gather_blocks(kv_own)
    q_blocks = gather_blocks(q_held, kv_own)
    crossed = [after(swap(q, far + k), kv_own) for k, q in enumerate(crossing)]
    o_held, *near = lax.optimization_barrier(
        (o_turned, *[p for pair in pairs[1 : far if assisted else count] for p in pair], q_blocks[far], kv_all[far])
    )[:-2]
    o_blocks = gather_blocks(o_held)
    attention = []

    def attend(*sent):
        attention.extend(
            call(
                partial(attend_body, count),
                [((tokens, qd), BF), ((tokens, qd), BF)],
                after(first_input, *sent), cosine, sine, *q_blocks, *kv_all,
                scalars=(here,),
                flops=2 * tokens * qd * (width + 2 * total),
                scratch=[grouped, keyed, keyed], limit=room,
            )
        )
        return attention[1]

    if assisted:
        completing, far_pairs = complete_pairs(crossed, attend)
    else:
        completing, far_pairs = attend(), []
    query, attended = attention
    near = [swap(p, 1 + k // 2) for k, p in enumerate(near)]
    all_pairs = [pairs[0], *zip(near[::2], near[1::2], strict=True), *far_pairs]
    gate_blocks, up_blocks = zip(*all_pairs, strict=True)
    x_one, input_two = call(
        partial(residual_body, width),
        [((tokens, wide), F32), ((tokens, wide), BF)],
        after(attended, completing), x_rel, gain_two, *o_blocks,
        flops=2 * tokens * qd * width,
    )

    joined = lambda blocks: jnp.concatenate(
        [jnp.pad(b, ((0, padded - block), (0, 0))) for b in blocks], axis=0
    )
    w_gate, w_up = joined(gate_blocks), joined(up_blocks)
    og_all = jnp.concatenate(gather_blocks(after(out_grad[0], o_blocks[far])), axis=0)

    reorder = lambda rows, j: jnp.concatenate(
        [rows[:, (i ^ j) * padded : ((i ^ j) + 1) * padded] for i in range(count)], axis=1
    )
    h2_blocks = gather_blocks(input_two)
    (h2_all,) = call(arrange_body, [((total, wide), BF)], *h2_blocks)
    grad_hidden = back(og_all, down_weight)
    gate, upward = dot(h2_all, w_gate), dot(h2_all, w_up)
    sigma = jax.nn.sigmoid(gate)
    silu_gate = gate * sigma
    hidden_act = (silu_gate * upward).astype(BF)
    grad_gate = (grad_hidden * upward * sigma * (1.0 + gate * (1.0 - sigma))).astype(BF)
    grad_up = (grad_hidden * silu_gate).astype(BF)
    dh2_part = (back(grad_gate, w_gate) + back(grad_up, w_up)).astype(BF)
    grad_in_two, dh2_sent = scatter_blocks(
        [reorder(dh2_part[j * tokens : (j + 1) * tokens], j) for j in range(count)]
    )
    grad_down = outer(hidden_act, og_all).astype(BF)
    rows_gu = up_to(block, 8 * reps)
    fit = lambda grad: jnp.pad(
        grad.reshape(count, padded, ff)[:, :rows_gu], ((0, 0), (0, max(rows_gu - padded, 0)), (0, 0))
    )
    grad_wgate, grad_wup = fit(outer(h2_all, grad_gate).astype(BF)), fit(outer(h2_all, grad_up).astype(BF))

    grad_x_one, grad_x_one_b, gain_two_grad, grad_attended = call(
        partial(residual_back_body, width),
        [((tokens, wide), F32), ((tokens, wide), BF), ((1, wide), F32), ((tokens, qd), BF)],
        grad_in_two, x_one, cot_rel, gain_two, *o_blocks,
        flops=2 * tokens * qd * width,
    )
    out_part = dot(hidden_act, down_weight)
    columns = lambda rows: [rows[:, j * padded : j * padded + block] for j in range(count)]
    dx_cols = exchange_blocks(columns(grad_x_one_b))
    h1_blocks = exchange_blocks(columns(after(first_input, hidden_act)))
    attended_blocks = gather_blocks(after(attended, hidden_act), grad_down)
    grad_q, dkv_part = call(
        partial(attend_back_body, count),
        [((tokens, qd), BF), ((total, 2 * kvd), BF)],
        query, attended, grad_attended, cosine, sine, *kv_all,
        scalars=(here,),
        flops=10 * tokens * qd * total,
        scratch=[grouped] * 3 + [keyed] * 2, limit=room,
    )
    dkv, dkv_sent = scatter_blocks([dkv_part[j * tokens : (j + 1) * tokens] for j in range(count)])
    out_sum, _ = scatter_blocks(
        [after(out_part[j * tokens : (j + 1) * tokens], grad_attended) for j in range(count)], dkv_sent
    )
    output = to_natural(x_one, block, padded) + out_sum
    (grad_kv,) = call(turn_keys_body, [((tokens, 2 * kvd), BF)], dkv, cosine, sine)

    rows_att = up_to(block, 8 * reps)
    pad_rows = lambda grad: jnp.pad(grad, ((0, rows_att - block), (0, 0)))
    dq_blocks = gather_blocks(after(grad_q, dkv_sent), grad_kv)
    dkv_blocks = gather_blocks(grad_kv)
    attended_all, h1_cols, dx_cols = [
        jnp.concatenate([after(blocks[0], grad_kv), *blocks[1:]], axis=0)
        for blocks in (attended_blocks, h1_blocks, dx_cols)
    ]
    dqkv_all = [jnp.concatenate(blocks, axis=0) for blocks in (dq_blocks, dkv_blocks)]
    grad_att = pad_rows(
        jnp.concatenate(
            [outer(h1_cols, rows).astype(BF) for rows in dqkv_all]
            + [outer(dx_cols, attended_all).astype(BF)],
            axis=1,
        )
    )
    att_share, trail = rep_reduce(grad_att, 0)
    gates = (dkv_sent, grad_kv, trail[-1])
    down_share, _ = rep_reduce(after(grad_down, dh2_sent), 0, 1, gates)
    gate_share, _ = rep_reduce(after(grad_wgate, dh2_sent), 1, 1, gates)
    up_share, _ = rep_reduce(after(grad_wup, dh2_sent), 1, 0, gates)

    cuts = (0, qd, qd + kvd, qd + 2 * kvd, 2 * qd + 2 * kvd)
    finish = lambda odd, own, arrived: call(
        partial(finish_body, cuts, True),
        [((block, qd), F32), ((block, kvd), F32), ((block, kvd), F32), ((qd, block), F32)],
        own,
        arrived,
        scalars=(odd.astype(jnp.int32)[None],),
    )
    sum_att, trail_back = rep_gather(att_share, 0, (), finish)
    gates = tuple(trail_back)
    plain = lambda rows, cols: lambda odd, own, arrived: call(
        partial(finish_body, (0, cols), False),
        [((rows, cols), F32)],
        own,
        arrived,
        scalars=(odd.astype(jnp.int32)[None],),
    )[0]
    sum_down, _ = rep_gather(down_share, 1, gates, plain(ff, width))
    shares = jnp.concatenate([gate_share, up_share], axis=2)
    blocks = exchange_blocks([shares[j] for j in range(count)])
    (sum_gate, _), (sum_up, _) = [
        rep_gather(
            jnp.concatenate(xor_blocks([b[:, k * ff : (k + 1) * ff] for b in blocks]), axis=1),
            1 - k, gates, plain(block, ff * count),
        )
        for k in range(2)
    ]
    grad_input, gain_one_grad, _ = call(
        partial(input_back_body, width, count),
        [((tokens, wide), F32), ((1, wide), F32), ((tokens, wide), F32)],
        after(grad_q, trail_back[0]), grad_kv, x_rel, grad_x_one, gain_one, *q_blocks, *kv_blocks,
        flops=2 * tokens * width * (qd + 2 * kvd),
    )
    grad_input = to_natural(grad_input, block, padded)

    both = jnp.concatenate([gain_one_grad, gain_two_grad], axis=0)
    arrived = exchange_blocks(columns(both))
    gain_sum = sum([after(b, trail_back[1 % len(trail_back)]) for b in arrived[1:]], arrived[0])
    late = [rows[:1, :1] for rows in (sum_gate, sum_up, sum_att[1])]
    arrived = [after(rep_swap(gain_sum, k), *late) for k in range(1, reps)]
    gain_sum = sum(arrived, gain_sum)
    return (
        output[None],
        grad_input[None],
        gain_sum[0],
        *sum_att,
        gain_sum[1],
        sum_gate,
        sum_up,
        sum_down,
    )


def solution(mesh):
    placed = (
        P("rep", "shard", None),
        P("rep", "shard", None),
        P("shard"),
        P("shard", None),
        P("shard", None),
        P("shard", None),
        P(None, "shard"),
        P("shard"),
        P("shard", None),
        P("shard", None),
        P("shard", None),
    )
    return jax.shard_map(
        local,
        mesh=mesh,
        in_specs=placed,
        out_specs=(
            P("rep", "shard", None),
            P("rep", "shard", None),
            P("shard"),
            P("shard", None),
            P("shard", None),
            P("shard", None),
            P(None, "shard"),
            P("shard"),
            P("shard", None),
            P("shard", None),
            P("shard", None),
        ),
        check_vma=False,
    )
```
